32 devices in a mesh: frame: 8 (over z, core), head: 4 (over y, x).
Axes of the slice: x: 2, y: 2, z: 4, core: 2. Of those that a mesh axis runs over, the one named last changes fastest.
Arguments:
- queries: bfloat16 [4096, 1024], P('frame', 'head'), may hold values from -6 to 6
- key_rows: bfloat16 [4096, 1024], P('frame', 'head'), may hold values from -6 to 6
- values: bfloat16 [4096, 1024], P('frame', 'head'), may hold values from -6 to 6
- gate_init: float32 [8, 128, 128], P('head'), may hold values from -0.5 to 0.5
- up_init: float32 [8, 128, 128], P('head'), may hold values from -0.5 to 0.5
- down_init: float32 [8, 128, 128], P('head'), may hold values from -0.5 to 0.5
- step_size: float32 [8], P('head'), may hold values from 0.1 to 1
- head_scale: float32 [8], P('head'), may hold values from 0.25 to 4
- out_gain: float32 [1024], P('head'), may hold values from 0.5 to 1.5
Outputs:
- layer_out: bfloat16 [4096, 1024], P('frame', 'head')
The draws below stay inside these ranges and needn't reach their ends.
All inputs are finite; a program needn't handle non-finite values.
Results may differ from the reference program's by a relative error of at most 0.012.
The reference program's roundings to bfloat16 on the way (of `probs`, `attended`, `query_norm` and `fast_out`) count: a program that leaves them out, or rounds other values in their place, can miss the bound.
Values may be sent and summed in bfloat16 or wider, within the bound.
A program may use at most 64 MiB of HBM per device.

```python
import math
import jax
import jax.numpy as jnp
from jax import lax

DH = 128
FWH = 128
FT = 512
NS_ITERS = 5
GROUPS = 2
HEADS = 8
TOKENS = 4096
N_FRAME = 8


def drawn_pair(key):
    base = jax.random.fold_in(key, 4111)
    width = HEADS * DH
    shape = (TOKENS, width)
    query_draw = jnp.clip(jax.random.normal(jax.random.fold_in(base, 1), shape, jnp.float32), -4.0, 4.0)
    key_draw = jnp.clip(jax.random.normal(jax.random.fold_in(base, 2), shape, jnp.float32), -4.0, 4.0)
    return (query_draw, key_draw)


def draw_queries(key, part):
    return drawn_pair(key)[0].astype(jnp.bfloat16)


def draw_key_rows(key, part):
    return drawn_pair(key)[1].astype(jnp.bfloat16)


def block_levels(key, dims, pieces, low, high):
    loudness = 1.0
    for axis_at, shards_of in pieces:
        steps = jax.random.uniform(jax.random.fold_in(jax.random.fold_in(key, 6), axis_at), (shards_of,), jnp.float32, low / len(pieces), high / len(pieces))
        loudness = loudness * jnp.repeat(jnp.exp(steps), dims[axis_at] // shards_of).reshape((-1,) + (1,) * (len(dims) - 1 - axis_at))
    return loudness


def centred(rng, dims, scale, limit, split=(), kind=jnp.bfloat16):
    values = scale * jax.random.normal(rng, dims, jnp.float32)
    if split:
        values = values * block_levels(rng, dims, split, -0.22, 0.18)
    return jnp.clip(values, -limit, limit).astype(kind)


def setup_inputs(seed: int = 0) -> dict:
    splits = jax.random.split(jax.random.key(seed), 10)
    queries = draw_queries(jax.random.fold_in(splits[9], 71), 0)
    key_rows = draw_key_rows(jax.random.fold_in(splits[9], 71), 0)
    values = centred(splits[2], (TOKENS, HEADS * DH), 1.0, 6.0, ((0, 8), (1, 4)))
    gate_init = centred(splits[3], (HEADS, DH, FWH), DH ** -0.5, 0.5, ((0, 4),), jnp.float32)
    up_init = centred(splits[4], (HEADS, DH, FWH), DH ** -0.5, 0.5, ((0, 4),), jnp.float32)
    down_init = centred(splits[5], (HEADS, FWH, DH), FWH ** -0.5, 0.5, ((0, 4),), jnp.float32)
    step_size = jnp.clip(jnp.exp(math.log(1.0) - 2.3025851 * jax.random.uniform(splits[6], (HEADS,), jnp.float32) ** block_levels(splits[6], (HEADS,), ((0, 4),), -0.2, 0.2)), 0.1, 1.0)
    head_scale = jnp.clip(jnp.exp(math.log(4.0) - 2.7725887 * jax.random.uniform(splits[7], (HEADS,), jnp.float32) ** block_levels(splits[7], (HEADS,), ((0, 4),), -0.2, 0.2)), 0.25, 4.0)
    out_gain = jnp.clip(1.0 + 0.1 * jax.random.normal(splits[8], (HEADS * DH,), jnp.float32), 0.5, 1.5)
    return {"queries": queries, "key_rows": key_rows, "values": values, "gate_init": gate_init, "up_init": up_init, "down_init": down_init, "step_size": step_size, "head_scale": head_scale, "out_gain": out_gain}


quintic_terms = (3.4445, -4.775, 2.0315)
highest = lax.Precision.HIGHEST

def rms_scale(rows_in, epsilon):
    mean_square = lax.optimization_barrier(jnp.mean(rows_in * rows_in, axis=-1, keepdims=True))
    return rows_in * lax.rsqrt(mean_square + epsilon)

def newton_schulz(gradient):
    flipped = gradient.shape[1] > gradient.shape[2]
    matrix = jnp.swapaxes(gradient, 1, 2) if flipped else gradient
    frobenius = jnp.sqrt(lax.optimization_barrier(jnp.sum(matrix * matrix, axis=(1, 2), keepdims=True)))
    matrix = matrix / (frobenius + 1e-07)
    for repeat_no in range(NS_ITERS):
        square = jnp.einsum('hij,hkj->hik', matrix, matrix, precision=highest)
        quartic = jnp.einsum('hij,hjk->hik', square, square, precision=highest)
        mixing = quintic_terms[1] * square + quintic_terms[2] * quartic
        matrix = quintic_terms[0] * matrix + jnp.einsum('hij,hjk->hik', mixing, matrix, precision=highest)
    return jnp.swapaxes(matrix, 1, 2) if flipped else matrix

def column_norms(weight):
    return jnp.sqrt(lax.optimization_barrier(jnp.sum(weight * weight, axis=1, keepdims=True)))

def fast_grads(weights, key_part, value_part):
    gate_w, up_w, down_w = weights
    key_f = key_part.astype(jnp.float32)
    value_f = value_part.astype(jnp.float32)
    gate = jnp.einsum('nhd,hdf->nhf', key_f, gate_w, precision=highest)
    upward = jnp.einsum('nhd,hdf->nhf', key_f, up_w, precision=highest)
    sigma = jax.nn.sigmoid(gate)
    active = gate * sigma
    hidden = active * upward
    back_hidden = -jnp.einsum('nhd,hfd->nhf', value_f, down_w, precision=highest)
    grad_down = -jnp.einsum('nhf,nhd->hfd', hidden, value_f, precision=highest)
    back_gate = back_hidden * upward * sigma * (1.0 + gate * (1.0 - sigma))
    back_up = back_hidden * active
    grad_gate = jnp.einsum('nhd,nhf->hdf', key_f, back_gate, precision=highest)
    grad_up = jnp.einsum('nhd,nhf->hdf', key_f, back_up, precision=highest)
    return (grad_gate, grad_up, grad_down)

def renewed(weights, gradients, step_size, targets):
    result = []
    for weight, gradient, target in zip(weights, gradients, targets):
        moved = weight - step_size[:, None, None] * newton_schulz(gradient)
        length = jnp.sqrt(lax.optimization_barrier(jnp.sum(moved * moved, axis=1, keepdims=True)))
        result.append(moved * (target / (length + 1e-06)))
    return tuple(result)

def fast_apply(weights, query_part, head_scale):
    gate_w, up_w, down_w = weights
    query_f = query_part.astype(jnp.float32)
    gate = jnp.einsum('nhd,hdf->nhf', query_f, gate_w, precision=highest)
    upward = jnp.einsum('nhd,hdf->nhf', query_f, up_w, precision=highest)
    hidden = jax.nn.silu(gate) * upward
    output = jnp.einsum('nhf,hfd->nhd', hidden, down_w, precision=highest)
    return (output * head_scale[None, :, None]).astype(jnp.bfloat16)

def reference(queries, key_rows, values, gate_init, up_init, down_init, step_size, head_scale, out_gain):
    frames = N_FRAME
    heads = HEADS
    grid_q = queries.reshape(frames, FT, heads, DH).transpose(0, 2, 1, 3)
    grid_k = key_rows.reshape(frames, FT, heads, DH).transpose(0, 2, 1, 3)
    grid_v = values.reshape(frames, FT, heads, DH).transpose(0, 2, 1, 3)
    score_scale = 1.0 / math.sqrt(DH)
    column = lax.broadcasted_iota(jnp.int32, (1, 2 * FT), 1)

    def one_pair(index):
        frame_no = index // heads
        head_no = index % heads
        prev_no = jnp.maximum(frame_no - 1, 0)
        query_part = grid_q[frame_no, head_no].astype(jnp.float32)
        key_all = jnp.concatenate([grid_k[prev_no, head_no], grid_k[frame_no, head_no]], axis=0).astype(jnp.float32)
        value_all = jnp.concatenate([grid_v[prev_no, head_no], grid_v[frame_no, head_no]], axis=0).astype(jnp.float32)
        scores = jnp.einsum('qd,kd->qk', query_part, key_all) * score_scale
        masked = jnp.logical_and(frame_no == 0, column < FT)
        scores = jnp.where(masked, -1e+30, scores)
        probs = jax.nn.softmax(scores, axis=-1).astype(jnp.bfloat16)
        probs = lax.optimization_barrier(probs).astype(jnp.float32)
        mixed = jnp.einsum('qk,kd->qd', probs, value_all)
        return rms_scale(mixed, 1e-06).astype(jnp.bfloat16)
    attended = lax.map(one_pair, jnp.arange(frames * heads, dtype=jnp.int32))
    attended = attended.reshape(frames, heads, FT, DH).transpose(0, 2, 1, 3).reshape(TOKENS, heads, DH)
    query_norm = rms_scale(queries.astype(jnp.float32).reshape(TOKENS, heads, DH), 1e-06).astype(jnp.bfloat16)
    value_grid = values.reshape(TOKENS, heads, DH)
    seg_len = TOKENS // GROUPS

    def per_head(packed):
        key_h, query_h, value_h, gate_w, up_w, down_w, step_h, scale_h = packed
        weights = (gate_w[None], up_w[None], down_w[None])
        targets = tuple((column_norms(weight) for weight in weights))
        outputs = []
        for segment in range(GROUPS):
            lower = segment * seg_len
            upper = lower + seg_len
            gradients = fast_grads(weights, key_h[lower:upper][:, None], value_h[lower:upper][:, None])
            weights = renewed(weights, gradients, step_h[None], targets)
            outputs.append(fast_apply(weights, query_h[lower:upper][:, None], scale_h[None])[:, 0])
        return jnp.concatenate(outputs, axis=0)
    fast_out = lax.map(per_head, (attended.transpose(1, 0, 2), query_norm.transpose(1, 0, 2), value_grid.transpose(1, 0, 2), gate_init, up_init, down_init, step_size, head_scale))
    fast_out = fast_out.transpose(1, 0, 2).reshape(TOKENS, heads * DH)
    combined = attended.reshape(TOKENS, heads * DH).astype(jnp.float32) + fast_out.astype(jnp.float32)
    total = lax.optimization_barrier(jnp.mean(combined * combined, axis=1, keepdims=True))
    return (combined * lax.rsqrt(total + 1e-05) * out_gain[None, :]).astype(jnp.bfloat16)
```

```python
import functools
import math

import jax
import jax.numpy as jnp
from jax import lax
from jax.experimental import pallas as pl
from jax.experimental.pallas import tpu as pltpu
from jax.sharding import PartitionSpec as P

NS_ITERS = 5
GROUPS = 2
MESH = pl.DeviceIdType.MESH
SENT = jnp.bfloat16
COARSE = 2
BF = jnp.bfloat16
F32 = jnp.float32
quintic_terms = (3.4445, -4.775, 2.0315)


def dot_nt(a, b):
    return lax.dot_general(a, b, (((1,), (1,)), ((), ())), preferred_element_type=F32)


def dot_nn(a, b):
    return lax.dot_general(a, b, (((1,), (0,)), ((), ())), preferred_element_type=F32)


def dot_tn(a, b):
    return lax.dot_general(a, b, (((0,), (0,)), ((), ())), preferred_element_type=F32)


def split(x):
    high = x.astype(BF)
    return high, (x - high.astype(F32)).astype(BF)


def side(*parts):
    return jnp.concatenate(parts, axis=1)


def over(*parts):
    return jnp.concatenate(parts, axis=0)


def sigmoid(v):
    return 0.5 * (1.0 + jnp.tanh(0.5 * v))


def parts_of(x, fine):
    return split(x) if fine else (x.astype(BF),)


def left(parts):
    return side(parts[0], parts[1], parts[0]) if len(parts) == 2 else parts[0]


def right(parts, axis):
    if len(parts) == 1:
        return parts[0]
    return jnp.concatenate((parts[0], parts[0], parts[1]), axis=axis)


def newton_schulz(grads):
    xs = []
    for m in grads:
        norm = jnp.sqrt(jnp.sum(m * m, keepdims=True))
        xs.append(m * (1.0 / (norm + 1e-07)))
    for step in range(NS_ITERS):
        fine = step >= COARSE
        halves = [parts_of(x, fine) for x in xs]
        squares = [dot_nt(left(h), right(h, 1)) for h in halves]
        sq = [parts_of(a, fine) for a in squares]
        quartics = [dot_nn(left(a), right(a, 0)) for a in sq]
        mixing = [quintic_terms[1] * a + quintic_terms[2] * q for a, q in zip(squares, quartics)]
        xs = [
            quintic_terms[0] * x + dot_nn(left(parts_of(b, fine)), right(h, 0))
            for x, b, h in zip(xs, mixing, halves)
        ]
    return xs


def lengths(m, axis):
    return jnp.sqrt(jnp.sum(m * m, axis=axis, keepdims=True))


AXES = (1, 1, 0)
ORDER = (2, 0, 1)


def kernel(
    dims,
    q_any, k_any, v_any, gate_any, up_any, down_any, step_any, scale_any,
    out_ref,
    qs, ks, vs, gate_ref, up_ref, down_ref, step_ref, scale_ref, local_sem,
    kp, here, before, mix, top, den, att, qn, comb, wb, wf, target, gp, hid, backs, cs, rz, tot, fw, by, wo, wr, part, others, frame_sem, head_sem, by_send, by_recv,
    kv_send, kv_recv, y_send, y_recv, att_send, att_recv, mate_send, mate_recv, fw_send, fw_recv,
    w_send, w_recv, head_send, head_recv,
):
    frames, nh, hd = dims
    rows, width = q_any.shape
    dh = width // hd
    half = frames // GROUPS
    mates = half // 2
    own = hd // 2
    p = lax.axis_index("frame")
    j = lax.axis_index("head")
    core = lax.rem(p, 2)
    seg = p // half
    rank = lax.rem(p, half) // 2
    pair = p + 1 - 2 * core
    has_prev = p > 0
    has_next = p < frames - 1
    prev_far = jnp.logical_and(core == 0, has_prev)
    next_far = jnp.logical_and(core == 1, has_next)

    def head_of(n, c):
        return (1 - c) * own + n if n < own else c * own + n - own

    def cols_of(h):
        return pl.ds(pl.multiple_of(h * dh, dh), dh)

    mine = pl.ds(core * own, own)
    moves = []
    for n in range(hd):
        cols = cols_of(head_of(n, core))
        for src, dst in ((k_any, ks), (q_any, qs), (v_any, vs)):
            moves.append((src.at[:, cols], dst.at[n]))
    moves += [
        (gate_any.at[mine], gate_ref), (up_any.at[mine], up_ref), (down_any.at[mine], down_ref),
        (step_any, step_ref), (scale_any, scale_ref),
    ]
    locals_ = [pltpu.make_async_copy(src, dst, local_sem.at[n]) for n, (src, dst) in enumerate(moves)]

    barrier = pltpu.get_barrier_semaphore()

    def signal(sem, frame_at, head_at):
        pl.semaphore_signal(sem, inc=1, device_id=(frame_at, head_at), device_id_type=MESH)

    def mate_at(step):
        return seg * half + 2 * lax.rem(rank + step, mates) + core

    def head_at(step):
        return lax.rem(j + step, nh)

    def flip(bit):
        return j + bit - 2 * bit * lax.rem(j // bit, 2)

    is_last = rank == mates - 1
    paired = nh & (nh - 1) == 0
    bits = [1 << k for k in range(nh.bit_length() - 1)]
    partners = [flip(bit) for bit in bits] if paired else [head_at(step) for step in range(1, nh)]

    def ring_signal(sem, reach):
        @pl.when(p + reach < frames)
        def _():
            signal(sem, p + reach, j)

        @pl.when(p >= reach)
        def _():
            signal(sem, p - reach, j)

    def ring_count(reach):
        return (p + reach < frames).astype(jnp.int32) + (p >= reach).astype(jnp.int32)

    signal(barrier, pair, j)

    @pl.when(next_far)
    def _():
        signal(barrier, p + 1, j)

    @pl.when(prev_far)
    def _():
        signal(barrier, p - 1, j)

    ring_signal(barrier, 2)
    for to in partners:
        signal(barrier, p, to)
    for copy in locals_:
        copy.start()
    far = prev_far.astype(jnp.int32) + next_far.astype(jnp.int32)
    pl.semaphore_wait(barrier, 1 + far + ring_count(2) + len(partners))

    frame_rounds = max((mates - 1).bit_length(), 0)
    head_rounds = len(bits) - 1 if paired else 0

    def frame_signal(k):
        ring_signal(frame_sem.at[k], 2 << k)

    def head_signal(k):
        for to in partners:
            signal(head_sem.at[k], p, to)

    def rounds():
        for k in range(frame_rounds):
            pl.semaphore_wait(frame_sem.at[k], ring_count(2 << k))
            if k + 1 < frame_rounds:
                frame_signal(k + 1)
        for k in range(head_rounds):
            pl.semaphore_wait(head_sem.at[k], len(partners))
            if k + 1 < head_rounds:
                head_signal(k + 1)

    ahead = jnp.minimum(p + 1, frames - 1)

    def kv_copy(n, which):
        cols = cols_of(head_of(n, 1 - core))
        src, dst = ((k_any, kp.at[n]), (v_any, vs.at[hd + n]))[which]
        return pltpu.make_async_remote_copy(
            src_ref=src.at[:, cols],
            dst_ref=dst,
            send_sem=kv_send.at[2 * n + which],
            recv_sem=kv_recv.at[2 * n + which],
            device_id=(ahead, j),
            device_id_type=MESH,
        )

    def y_copy(i):
        return pltpu.make_async_remote_copy(
            src_ref=v_any.at[:, pl.ds(i * dh, dh)],
            dst_ref=vs.at[2 * hd + i],
            send_sem=y_send.at[i],
            recv_sem=y_recv.at[i],
            device_id=(pair, j),
            device_id_type=MESH,
        )

    def att_copy(i):
        return pltpu.make_async_remote_copy(
            src_ref=att.at[i],
            dst_ref=att.at[hd + i],
            send_sem=att_send.at[i],
            recv_sem=att_recv.at[i],
            device_id=(pair, j),
            device_id_type=MESH,
        )

    @pl.when(has_next)
    def _():
        for n in range(hd):
            for which in range(2):
                kv_copy(n, which).start()

    @pl.when(core == 1)
    def _():
        for i in range(own):
            y_copy(i).start()

    if frame_rounds:
        frame_signal(0)
    if head_rounds:
        head_signal(0)

    factor = math.log2(math.e) / math.sqrt(dh)

    block = min(rows, 256)

    for copy in locals_:
        copy.wait()

    def exps(q, keys):
        scores = dot_nt(q, keys) * factor
        high = jnp.max(scores, axis=1, keepdims=True)
        e = jnp.exp2(scores - high)
        return e, high, jnp.sum(e, axis=1, keepdims=True)

    for n in range(hd):
        for r in range(0, rows, block):
            rs = slice(r, r + block)
            e, t, d = exps(qs[n, rs], ks[n])
            here[n, rs] = e
            top[n, rs] = t
            den[n, rs] = d
        qf = qs[n].astype(F32)
        mean = jnp.mean(qf * qf, axis=1, keepdims=True)
        qn[n] = (qf * lax.rsqrt(mean + 1e-06)).astype(BF)
    for i in range(own):
        for m, ref in enumerate((gate_ref, up_ref, down_ref)):
            w = ref[i]
            w = w.T if AXES[m] else w
            wf[i, m] = w
            target[i, m] = jnp.broadcast_to(lengths(w, AXES[m]), w.shape)
            high, low = split(w)
            wb[0, i, m] = side(high, low)

    def weigh(n):
        @pl.when(has_prev)
        def _():
            kv_copy(n, 0).wait_recv()
            for r in range(0, rows, block):
                rs = slice(r, r + block)
                e, t, d = exps(qs[n, rs], kp[n])
                t0 = top[n, rs]
                high = jnp.maximum(t, t0)
                a, b = jnp.exp2(t0 - high), jnp.exp2(t - high)
                inv = 1.0 / (den[n, rs] * a + d * b)
                before[n, rs] = (e * (b * inv)).astype(BF)
                probs = (here[n, rs] * (a * inv)).astype(BF)
                mix[n, rs] = dot_nn(probs, vs[n])

        @pl.when(jnp.logical_not(has_prev))
        def _():
            for r in range(0, rows, block):
                rs = slice(r, r + block)
                probs = (here[n, rs] * (1.0 / den[n, rs])).astype(BF)
                mix[n, rs] = dot_nn(probs, vs[n])

    def attend(n):
        @pl.when(has_prev)
        def _():
            kv_copy(n, 1).wait_recv()
            mix[n] = mix[n] + dot_nn(before[n], vs[hd + n])

        m = mix[n]
        mean = jnp.mean(m * m, axis=1, keepdims=True)
        att[n] = (m * lax.rsqrt(mean + 1e-06)).astype(BF)

    for n in range(own):
        weigh(n)
        attend(n)
        att_copy(n).start()
    rounds()

    def mate_copy(step, i, m):
        return pltpu.make_async_remote_copy(
            src_ref=cs.at[i, m],
            dst_ref=rz.at[step - 1, i, m],
            send_sem=mate_send.at[step - 1, i * 3 + m],
            recv_sem=mate_recv.at[step - 1, i * 3 + m],
            device_id=(mate_at(step), j),
            device_id_type=MESH,
        )

    beyond = jnp.minimum(p + 2, frames - 1)

    def fw_copy(src, frame_at, k, i, m):
        return pltpu.make_async_remote_copy(
            src_ref=src,
            dst_ref=fw.at[i, m],
            send_sem=fw_send.at[k, i * 3 + m],
            recv_sem=fw_recv.at[i * 3 + m],
            device_id=(frame_at, j),
            device_id_type=MESH,
        )

    def fw_direct(k, i, m):
        return fw_copy(cs.at[own + i, m], half + 2 * k + core, k, i, m)

    def relay(i, m):
        return fw_copy(fw.at[i, m], beyond, 0, i, m)

    def aside(i, m):
        return pltpu.make_async_remote_copy(
            src_ref=cs.at[own + i, m],
            dst_ref=by.at[i, m],
            send_sem=by_send.at[i * 3 + m],
            recv_sem=by_recv.at[i * 3 + m],
            device_id=(pair, j),
            device_id_type=MESH,
        )

    def behalf(i, m):
        return fw_copy(by.at[i, m], ahead, mates, i, m)

    def fw_sends(c, i, m):
        if m == ORDER[-1]:
            return [fw_direct(k, i, m) for k in reversed(range(mates))]
        if c == 1:
            return [fw_direct(0, i, m)]
        return [fw_direct(k, i, m) for k in reversed(range(1, mates))] + [aside(i, m)]

    relays = jnp.logical_and(core == 1, p < frames - 2)
    closes = jnp.logical_and(seg == 0, is_last)

    def w_copy(i, m):
        return pltpu.make_async_remote_copy(
            src_ref=wo.at[i, m],
            dst_ref=wr.at[i, m],
            send_sem=w_send.at[i * 3 + m],
            recv_sem=w_recv.at[i * 3 + m],
            device_id=(pair, j),
            device_id_type=MESH,
        )

    always = p < frames

    def fast_grads(state, i, sets, finish):
        @pl.when(always)
        def _():
            total = None
            for k, (xi, yi) in enumerate(sets):
                x = att[xi]
                xx = side(x, x)
                gate = dot_nt(wb[state, i, 0], xx)
                upward = dot_nt(wb[state, i, 1], xx)
                sig = sigmoid(gate)
                active = gate * sig
                hid[k, 0] = active
                hid[k, 1] = upward * sig * (1.0 + gate * (1.0 - sig))
                d = dot_nn((active * upward).astype(BF), vs[yi])
                total = d if total is None else total + d
            finish(i, 2, -total)

        @pl.when(always)
        def _():
            total = None
            for k, (xi, yi) in enumerate(sets):
                y = vs[yi]
                back = -dot_nt(wb[state, i, 2], side(y, y))
                backs[k] = (back * hid[k, 0]).astype(BF)
                d = dot_nn((back * hid[k, 1]).astype(BF), att[xi])
                total = d if total is None else total + d
            finish(i, 0, total)

        @pl.when(always)
        def _():
            total = None
            for k, (xi, yi) in enumerate(sets):
                d = dot_nn(backs[k], att[xi])
                total = d if total is None else total + d
            finish(i, 1, total)

    def keep(i, m, value):
        gp[i, m] = value

    def mate_start(i, m):
        for step in range(1, mates):
            mate_copy(step, i, m).start()

    def with_mates(i, m, total):
        for step in range(1, mates):
            mate_copy(step, i, m).wait_recv()
            total = total + rz[step - 1, i, m].astype(F32)
        return total

    def share(i, m, value):
        tot[i, m] = value
        cs[i, m] = value.astype(SENT)
        mate_start(i, m)

    def share_late(i, m, value):
        value = value + gp[i, m]
        cs[i, m] = value.astype(SENT)
        tot[i, m] = value

        @pl.when(jnp.logical_not(is_last))
        def _():
            mate_start(i, m)

        @pl.when(is_last)
        def _():
            total = with_mates(i, m, tot[i, m])
            tot[i, m] = total
            cs[own + i, m] = total.astype(SENT)

        for c in range(2):
            @pl.when(jnp.logical_and(is_last, core == c))
            def _(c=c):
                for copy in fw_sends(c, i, m):
                    copy.start()

    def pair_wait(i):
        att_copy(i).wait_recv()

        @pl.when(core == 0)
        def _():
            y_copy(i).wait_recv()

    hold = prev_far.astype(jnp.int32)

    def pair_set(i):
        return hd + i, 2 * hd + i - core * (hd - own)

    def early_set(i):
        return own + i + hold * (hd - own), own + i + hold * (2 * hd - own)

    def late_set(i):
        x, y = pair_set(i)
        return x + hold * (own + i - x), y + hold * (own + i - y)

    opening = seg == 0
    first_pair = jnp.logical_and(opening, prev_far)

    @pl.when(first_pair)
    def _():
        for i in range(own):
            pair_wait(i)
            fast_grads(0, i, [early_set(i)], keep)

    for n in range(own, hd):
        weigh(n)
        attend(n)

    @pl.when(jnp.logical_and(opening, jnp.logical_not(prev_far)))
    def _():
        for i in range(own):
            fast_grads(0, i, [early_set(i)], keep)
            pair_wait(i)

    for s in range(GROUPS):
        @pl.when(seg == s)
        def _(s=s):
            for i in range(own):
                if s == 0:
                    fast_grads(s, i, [late_set(i)], share_late)
                else:
                    pair_wait(i)
                    fast_grads(s, i, [(own + i, own + i), pair_set(i)], share)
            if s == 0:
                @pl.when(jnp.logical_and(is_last, core == 1))
                def _():
                    for m in ORDER[:-1]:
                        for i in range(own):
                            aside(i, m).wait_recv()
                            behalf(i, m).start()

                @pl.when(is_last)
                def _():
                    for m in ORDER:
                        for i in range(own):
                            mate_start(i, m)

                @pl.when(jnp.logical_not(is_last))
                def _():
                    for m in ORDER:
                        for i in range(own):
                            tot[i, m] = with_mates(i, m, tot[i, m])
            else:
                for m in ORDER:
                    for i in range(own):
                        tot[i, m] = with_mates(i, m, tot[i, m])

        if s == 0:
            @pl.when(seg > 0)
            def _():
                for m in ORDER:
                    for i in range(own):
                        relay(i, m).wait_recv()
                        if m != ORDER[-1]:
                            @pl.when(relays)
                            def _(i=i, m=m):
                                relay(i, m).start()

                        tot[i, m] = fw[i, m].astype(F32)

        @pl.when(seg >= s)
        def _(s=s):
            for i in range(own):
                rate = step_ref[core * own + i]
                ortho = newton_schulz([tot[i, m] for m in range(3)])
                for m in range(3):
                    moved = wf[i, m] - rate * ortho[m]
                    w = moved * (target[i, m] / (lengths(moved, AXES[m]) + 1e-06))
                    high, low = split(w)
                    wo[i, m] = high
                    if s < GROUPS - 1:
                        wf[i, m] = w
                        wb[s + 1, i, m] = side(high, low)

            @pl.when(seg == s)
            def _():
                for i in range(own):
                    for m in range(3):
                        w_copy(i, m).start()

    ones = jnp.ones((8, dh), BF)
    sums = jnp.zeros((8, rows), F32)
    for n in [*range(own, hd), *range(own)]:
        if n < own:
            for m in range(3):
                w_copy(n, m).wait_recv()
        final = wr if n < own else wo
        i = n if n < own else n - own
        x = qn[n]
        gate = dot_nt(x, final[i, 0])
        upward = dot_nt(x, final[i, 1])
        hidden = (gate * sigmoid(gate) * upward).astype(BF)
        out = dot_nn(hidden, final[i, 2])
        fast = (out * scale_ref[head_of(n, core)]).astype(BF)
        both = att[n].astype(F32) + fast.astype(F32)
        comb[n] = both
        high, low = split(both * both)
        sums = sums + dot_nt(side(ones, ones), side(high, low))
    sums = jnp.maximum(sums, 0.0)
    part[...] = sums[:1]

    def head_copy(step):
        return pltpu.make_async_remote_copy(
            src_ref=part,
            dst_ref=others.at[step - 1],
            send_sem=head_send.at[step - 1],
            recv_sem=head_recv.at[step - 1],
            device_id=(p, head_at(step)),
            device_id_type=MESH,
        )

    for step in range(1, nh):
        head_copy(step).start()
    total = sums[:1]
    for step in range(1, nh):
        head_copy(step).wait_recv()
        total = total + others[step - 1]
    total = jnp.broadcast_to(total, (8, rows))
    high, low = split(lax.rsqrt(total / (width * nh) + 1e-05))
    eighths = jnp.full((16, dh), 0.125, BF)
    inverse = dot_tn(over(high.astype(F32), low.astype(F32)).astype(BF), eighths)
    for n in range(hd):
        out_ref[:, cols_of(head_of(n, core))] = comb[n] * inverse

    for step in range(1, nh):
        head_copy(step).wait_send()

    @pl.when(has_next)
    def _():
        for n in range(hd):
            for which in range(2):
                kv_copy(n, which).wait_send()

    @pl.when(core == 1)
    def _():
        for i in range(own):
            y_copy(i).wait_send()

    for i in range(own):
        att_copy(i).wait_send()
        for m in range(3):
            w_copy(i, m).wait_send()
            for step in range(1, mates):
                mate_copy(step, i, m).wait_send()
    for c in range(2):
        @pl.when(jnp.logical_and(closes, core == c))
        def _(c=c):
            for i in range(own):
                for m in range(3):
                    for copy in fw_sends(c, i, m):
                        copy.wait_send()
                    if c == 1 and m != ORDER[-1]:
                        behalf(i, m).wait_send()

    @pl.when(jnp.logical_and(seg > 0, relays))
    def _():
        for i in range(own):
            for m in ORDER[:-1]:
                relay(i, m).wait_send()


def shards(
    queries, key_rows, values, gate_init, up_init, down_init, step_size, head_scale, out_gain
):
    rows, width = queries.shape
    hd, dh, fwh = gate_init.shape
    frames, nh = lax.axis_size("frame"), lax.axis_size("head")
    mates = frames // GROUPS // 2
    own = hd // 2
    dma = pltpu.SemaphoreType.DMA
    vmem = pl.BlockSpec(memory_space=pltpu.VMEM)
    scaled = pl.pallas_call(
        functools.partial(kernel, (frames, nh, hd)),
        out_shape=pltpu.VMEM((rows, width), F32),
        in_specs=[pl.BlockSpec(memory_space=pl.ANY)] * 8,
        out_specs=vmem,
        scratch_shapes=[
            pltpu.VMEM((hd, rows, dh), BF),
            pltpu.VMEM((hd, rows, dh), BF),
            pltpu.VMEM((2 * hd + own, rows, dh), BF),
            pltpu.VMEM((own, dh, fwh), F32),
            pltpu.VMEM((own, dh, fwh), F32),
            pltpu.VMEM((own, fwh, dh), F32),
            pltpu.SMEM((hd,), F32),
            pltpu.SMEM((hd,), F32),
            dma((3 * hd + 5,)),
            pltpu.VMEM((hd, rows, dh), BF),
            pltpu.VMEM((hd, rows, rows), F32),
            pltpu.VMEM((hd, rows, rows), BF),
            pltpu.VMEM((hd, rows, dh), F32),
            pltpu.VMEM((hd, rows, 1), F32),
            pltpu.VMEM((hd, rows, 1), F32),
            pltpu.VMEM((hd + own, rows, dh), BF),
            pltpu.VMEM((hd, rows, dh), BF),
            pltpu.VMEM((hd, rows, dh), F32),
            pltpu.VMEM((GROUPS, own, 3, dh, 2 * fwh), BF),
            pltpu.VMEM((own, 3, dh, fwh), F32),
            pltpu.VMEM((own, 3, dh, fwh), F32),
            pltpu.VMEM((own, 3, dh, fwh), F32),
            pltpu.VMEM((2, 2, fwh, rows), F32),
            pltpu.VMEM((2, fwh, rows), BF),
            pltpu.VMEM((2 * own, 3, dh, fwh), SENT),
            pltpu.VMEM((max(mates - 1, 1), own, 3, dh, fwh), SENT),
            pltpu.VMEM((own, 3, dh, fwh), F32),
            pltpu.VMEM((own, 3, dh, fwh), SENT),
            pltpu.VMEM((own, 3, dh, fwh), SENT),
            pltpu.VMEM((own, 3, dh, fwh), BF),
            pltpu.VMEM((own, 3, dh, fwh), BF),
            pltpu.VMEM((1, rows), F32),
            pltpu.VMEM((max(nh - 1, 1), 1, rows), F32),
            pltpu.SemaphoreType.REGULAR((max(mates.bit_length(), 1),)),
            pltpu.SemaphoreType.REGULAR((max(nh.bit_length(), 1),)),
            dma((own * 3,)), dma((own * 3,)),
            dma((2 * hd,)), dma((2 * hd,)),
            dma((own,)), dma((own,)),
            dma((own,)), dma((own,)),
            dma((max(mates - 1, 1), own * 3)), dma((max(mates - 1, 1), own * 3)),
            dma((mates + 1, own * 3)), dma((own * 3,)),
            dma((own * 3,)), dma((own * 3,)),
            dma((max(nh - 1, 1),)), dma((max(nh - 1, 1),)),
        ],
        compiler_params=pltpu.CompilerParams(
            collective_id=0, has_side_effects=True, vmem_limit_bytes=56 * 1024 * 1024
        ),
    )(
        queries, key_rows, values, gate_init, up_init, down_init, step_size, head_scale,
    )
    return (scaled * out_gain[None, :]).astype(BF)


def solution(mesh):
    in_specs = (
        P("frame", "head"),
        P("frame", "head"),
        P("frame", "head"),
        P("head", None, None),
        P("head", None, None),
        P("head", None, None),
        P("head"),
        P("head"),
        P("head"),
    )
    return jax.shard_map(
        shards, mesh=mesh, in_specs=in_specs, out_specs=P("frame", "head"), check_vma=False
    )
```

```python
import functools
import math

import jax
import jax.numpy as jnp
from jax import lax
from jax.experimental import pallas as pl
from jax.experimental.pallas import tpu as pltpu
from jax.sharding import PartitionSpec as P

NS_ITERS = 5
GROUPS = 2
MESH = pl.DeviceIdType.MESH
SENT = jnp.bfloat16
COARSE = 2
BF = jnp.bfloat16
F32 = jnp.float32
quintic_terms = (3.4445, -4.775, 2.0315)


def dot_nt(a, b):
    return lax.dot_general(a, b, (((1,), (1,)), ((), ())), preferred_element_type=F32)


def dot_nn(a, b):
    return lax.dot_general(a, b, (((1,), (0,)), ((), ())), preferred_element_type=F32)


def dot_tn(a, b):
    return lax.dot_general(a, b, (((0,), (0,)), ((), ())), preferred_element_type=F32)


def split(x):
    high = x.astype(BF)
    return high, (x - high.astype(F32)).astype(BF)


def side(*parts):
    return jnp.concatenate(parts, axis=1)


def over(*parts):
    return jnp.concatenate(parts, axis=0)


def sigmoid(v):
    return 0.5 * (1.0 + jnp.tanh(0.5 * v))


def parts_of(x, fine):
    return split(x) if fine else (x.astype(BF),)


def left(parts):
    return side(parts[0], parts[1], parts[0]) if len(parts) == 2 else parts[0]


def right(parts, axis):
    if len(parts) == 1:
        return parts[0]
    return jnp.concatenate((parts[0], parts[0], parts[1]), axis=axis)


def newton_schulz(grads):
    xs = []
    for m in grads:
        norm = jnp.sqrt(jnp.sum(m * m, keepdims=True))
        xs.append(m * (1.0 / (norm + 1e-07)))
    for step in range(NS_ITERS):
        fine = step >= COARSE
        halves = [parts_of(x, fine) for x in xs]
        squares = [dot_nt(left(h), right(h, 1)) for h in halves]
        sq = [parts_of(a, fine) for a in squares]
        quartics = [dot_nn(left(a), right(a, 0)) for a in sq]
        mixing = [quintic_terms[1] * a + quintic_terms[2] * q for a, q in zip(squares, quartics)]
        xs = [
            quintic_terms[0] * x + dot_nn(left(parts_of(b, fine)), right(h, 0))
            for x, b, h in zip(xs, mixing, halves)
        ]
    return xs


def lengths(m, axis):
    return jnp.sqrt(jnp.sum(m * m, axis=axis, keepdims=True))


AXES = (1, 1, 0)
ORDER = (2, 0, 1)


def kernel(
    dims,
    q_any, k_any, v_any, gate_any, up_any, down_any, step_any, scale_any,
    out_ref,
    qs, ks, vs, gate_ref, up_ref, down_ref, step_ref, scale_ref, local_sem,
    kp, here, before, mix, top, den, att, qn, comb, wb, wf, target, gp, hid, backs, cs, rz, tot, fw, wo, wr, part, others, frame_sem, head_sem,
    kv_send, kv_recv, y_send, y_recv, att_send, att_recv, mate_send, mate_recv, fw_send, fw_recv,
    w_send, w_recv, head_send, head_recv,
):
    frames, nh, hd = dims
    rows, width = q_any.shape
    dh = width // hd
    half = frames // GROUPS
    mates = half // 2
    own = hd // 2
    p = lax.axis_index("frame")
    j = lax.axis_index("head")
    core = lax.rem(p, 2)
    seg = p // half
    rank = lax.rem(p, half) // 2
    pair = p + 1 - 2 * core
    has_prev = p > 0
    has_next = p < frames - 1
    prev_far = jnp.logical_and(core == 0, has_prev)
    next_far = jnp.logical_and(core == 1, has_next)

    def head_of(n, c):
        return (1 - c) * own + n if n < own else c * own + n - own

    def cols_of(h):
        return pl.ds(pl.multiple_of(h * dh, dh), dh)

    mine = pl.ds(core * own, own)
    moves = []
    for n in range(hd):
        cols = cols_of(head_of(n, core))
        for src, dst in ((k_any, ks), (q_any, qs), (v_any, vs)):
            moves.append((src.at[:, cols], dst.at[n]))
    moves += [
        (gate_any.at[mine], gate_ref), (up_any.at[mine], up_ref), (down_any.at[mine], down_ref),
        (step_any, step_ref), (scale_any, scale_ref),
    ]
    locals_ = [pltpu.make_async_copy(src, dst, local_sem.at[n]) for n, (src, dst) in enumerate(moves)]

    barrier = pltpu.get_barrier_semaphore()

    def signal(sem, frame_at, head_at):
        pl.semaphore_signal(sem, inc=1, device_id=(frame_at, head_at), device_id_type=MESH)

    def mate_at(step):
        return seg * half + 2 * lax.rem(rank + step, mates) + core

    def head_at(step):
        return lax.rem(j + step, nh)

    def flip(bit):
        return j + bit - 2 * bit * lax.rem(j // bit, 2)

    is_last = rank == mates - 1
    paired = nh & (nh - 1) == 0
    bits = [1 << k for k in range(nh.bit_length() - 1)]
    partners = [flip(bit) for bit in bits] if paired else [head_at(step) for step in range(1, nh)]

    def ring_signal(sem, reach):
        @pl.when(p + reach < frames)
        def _():
            signal(sem, p + reach, j)

        @pl.when(p >= reach)
        def _():
            signal(sem, p - reach, j)

    def ring_count(reach):
        return (p + reach < frames).astype(jnp.int32) + (p >= reach).astype(jnp.int32)

    signal(barrier, pair, j)

    @pl.when(next_far)
    def _():
        signal(barrier, p + 1, j)

    @pl.when(prev_far)
    def _():
        signal(barrier, p - 1, j)

    ring_signal(barrier, 2)
    for to in partners:
        signal(barrier, p, to)
    for copy in locals_:
        copy.start()
    far = prev_far.astype(jnp.int32) + next_far.astype(jnp.int32)
    pl.semaphore_wait(barrier, 1 + far + ring_count(2) + len(partners))

    frame_rounds = max((mates - 1).bit_length(), 0)
    head_rounds = len(bits) - 1 if paired else 0

    def frame_signal(k):
        ring_signal(frame_sem.at[k], 2 << k)

    def head_signal(k):
        for to in partners:
            signal(head_sem.at[k], p, to)

    def rounds():
        for k in range(frame_rounds):
            pl.semaphore_wait(frame_sem.at[k], ring_count(2 << k))
            if k + 1 < frame_rounds:
                frame_signal(k + 1)
        for k in range(head_rounds):
            pl.semaphore_wait(head_sem.at[k], len(partners))
            if k + 1 < head_rounds:
                head_signal(k + 1)

    ahead = jnp.minimum(p + 1, frames - 1)

    def kv_copy(n, which):
        cols = cols_of(head_of(n, 1 - core))
        src, dst = ((k_any, kp.at[n]), (v_any, vs.at[hd + n]))[which]
        return pltpu.make_async_remote_copy(
            src_ref=src.at[:, cols],
            dst_ref=dst,
            send_sem=kv_send.at[2 * n + which],
            recv_sem=kv_recv.at[2 * n + which],
            device_id=(ahead, j),
            device_id_type=MESH,
        )

    def y_copy(i):
        return pltpu.make_async_remote_copy(
            src_ref=v_any.at[:, pl.ds(i * dh, dh)],
            dst_ref=vs.at[2 * hd + i],
            send_sem=y_send.at[i],
            recv_sem=y_recv.at[i],
            device_id=(pair, j),
            device_id_type=MESH,
        )

    def att_copy(i):
        return pltpu.make_async_remote_copy(
            src_ref=att.at[i],
            dst_ref=att.at[hd + i],
            send_sem=att_send.at[i],
            recv_sem=att_recv.at[i],
            device_id=(pair, j),
            device_id_type=MESH,
        )

    @pl.when(has_next)
    def _():
        for which in range(2):
            for n in range(hd):
                kv_copy(n, which).start()

    @pl.when(core == 1)
    def _():
        for i in range(own):
            y_copy(i).start()

    if frame_rounds:
        frame_signal(0)
    if head_rounds:
        head_signal(0)

    factor = math.log2(math.e) / math.sqrt(dh)

    block = min(rows, 256)

    for copy in locals_:
        copy.wait()

    def exps(q, keys):
        scores = dot_nt(q, keys) * factor
        high = jnp.max(scores, axis=1, keepdims=True)
        e = jnp.exp2(scores - high)
        return e, high, jnp.sum(e, axis=1, keepdims=True)

    for n in range(hd):
        for r in range(0, rows, block):
            rs = slice(r, r + block)
            e, t, d = exps(qs[n, rs], ks[n])
            here[n, rs] = e
            top[n, rs] = t
            den[n, rs] = d
        qf = qs[n].astype(F32)
        mean = jnp.mean(qf * qf, axis=1, keepdims=True)
        qn[n] = (qf * lax.rsqrt(mean + 1e-06)).astype(BF)
    for i in range(own):
        for m, ref in enumerate((gate_ref, up_ref, down_ref)):
            w = ref[i]
            w = w.T if AXES[m] else w
            wf[i, m] = w
            target[i, m] = jnp.broadcast_to(lengths(w, AXES[m]), w.shape)
            high, low = split(w)
            wb[0, i, m] = side(high, low)

    def weigh(n):
        @pl.when(has_prev)
        def _():
            kv_copy(n, 0).wait_recv()
            for r in range(0, rows, block):
                rs = slice(r, r + block)
                e, t, d = exps(qs[n, rs], kp[n])
                t0 = top[n, rs]
                high = jnp.maximum(t, t0)
                a, b = jnp.exp2(t0 - high), jnp.exp2(t - high)
                inv = 1.0 / (den[n, rs] * a + d * b)
                before[n, rs] = (e * (b * inv)).astype(BF)
                probs = (here[n, rs] * (a * inv)).astype(BF)
                mix[n, rs] = dot_nn(probs, vs[n])

        @pl.when(jnp.logical_not(has_prev))
        def _():
            for r in range(0, rows, block):
                rs = slice(r, r + block)
                probs = (here[n, rs] * (1.0 / den[n, rs])).astype(BF)
                mix[n, rs] = dot_nn(probs, vs[n])

    def attend(n):
        @pl.when(has_prev)
        def _():
            kv_copy(n, 1).wait_recv()
            mix[n] = mix[n] + dot_nn(before[n], vs[hd + n])

        m = mix[n]
        mean = jnp.mean(m * m, axis=1, keepdims=True)
        att[n] = (m * lax.rsqrt(mean + 1e-06)).astype(BF)

    for n in range(hd):
        weigh(n)
    for n in range(own):
        attend(n)
        att_copy(n).start()
    rounds()

    def mate_copy(step, i, m):
        return pltpu.make_async_remote_copy(
            src_ref=cs.at[i, m],
            dst_ref=rz.at[step - 1, i, m],
            send_sem=mate_send.at[step - 1, i * 3 + m],
            recv_sem=mate_recv.at[step - 1, i * 3 + m],
            device_id=(mate_at(step), j),
            device_id_type=MESH,
        )

    beyond = jnp.minimum(p + 2, frames - 1)

    def fw_copy(src, frame_at, k, i, m):
        return pltpu.make_async_remote_copy(
            src_ref=src,
            dst_ref=fw.at[i, m],
            send_sem=fw_send.at[k, i * 3 + m],
            recv_sem=fw_recv.at[i * 3 + m],
            device_id=(frame_at, j),
            device_id_type=MESH,
        )

    def fw_direct(k, i, m):
        return fw_copy(cs.at[own + i, m], half + 2 * k + core, k, i, m)

    def relay(i, m):
        return fw_copy(fw.at[i, m], beyond, 0, i, m)

    def fw_sends(c, m):
        near = [(0, i, m) for i in range(own)]
        if c == 1 or m == ORDER[0]:
            return near
        far = [(k, i, m) for i in range(own) for k in reversed(range(1, mates))]
        if m != ORDER[-1]:
            return far
        return far + [(0, i, ORDER[1]) for i in range(own)] + near

    def relayed(c):
        return ORDER if c == 1 else ORDER[:1]

    relays = [jnp.logical_and(core == c, p < frames - 2) for c in range(2)]
    closes = jnp.logical_and(seg == 0, is_last)

    def w_copy(i, m):
        return pltpu.make_async_remote_copy(
            src_ref=wo.at[i, m],
            dst_ref=wr.at[i, m],
            send_sem=w_send.at[i * 3 + m],
            recv_sem=w_recv.at[i * 3 + m],
            device_id=(pair, j),
            device_id_type=MESH,
        )

    always = p < frames

    def fast_grads(state, i, sets, finish):
        @pl.when(always)
        def _():
            total = None
            for k, (xi, yi) in enumerate(sets):
                x = att[xi]
                xx = side(x, x)
                gate = dot_nt(wb[state, i, 0], xx)
                upward = dot_nt(wb[state, i, 1], xx)
                sig = sigmoid(gate)
                active = gate * sig
                hid[k, 0] = active
                hid[k, 1] = upward * sig * (1.0 + gate * (1.0 - sig))
                d = dot_nn((active * upward).astype(BF), vs[yi])
                total = d if total is None else total + d
            finish(i, 2, -total)

        @pl.when(always)
        def _():
            total = None
            for k, (xi, yi) in enumerate(sets):
                y = vs[yi]
                back = -dot_nt(wb[state, i, 2], side(y, y))
                backs[k] = (back * hid[k, 0]).astype(BF)
                d = dot_nn((back * hid[k, 1]).astype(BF), att[xi])
                total = d if total is None else total + d
            finish(i, 0, total)

        @pl.when(always)
        def _():
            total = None
            for k, (xi, yi) in enumerate(sets):
                d = dot_nn(backs[k], att[xi])
                total = d if total is None else total + d
            finish(i, 1, total)

    def keep(i, m, value):
        gp[i, m] = value

    def mate_start(i, m):
        for step in range(1, mates):
            mate_copy(step, i, m).start()

    def with_mates(i, m, total):
        for step in range(1, mates):
            mate_copy(step, i, m).wait_recv()
            total = total + rz[step - 1, i, m].astype(F32)
        return total

    def share(i, m, value):
        tot[i, m] = value
        cs[i, m] = value.astype(SENT)
        mate_start(i, m)

    def share_late(i, m, value):
        value = value + gp[i, m]
        cs[i, m] = value.astype(SENT)
        tot[i, m] = value

        @pl.when(jnp.logical_not(is_last))
        def _():
            mate_start(i, m)

        @pl.when(is_last)
        def _():
            total = with_mates(i, m, tot[i, m])
            tot[i, m] = total
            cs[own + i, m] = total.astype(SENT)

        if i == own - 1:
            for c in range(2):
                @pl.when(jnp.logical_and(is_last, core == c))
                def _(c=c):
                    for at in fw_sends(c, m):
                        fw_direct(*at).start()

    def pair_wait(i):
        att_copy(i).wait_recv()

        @pl.when(core == 0)
        def _():
            y_copy(i).wait_recv()

    hold = prev_far.astype(jnp.int32)

    def pair_set(i):
        return hd + i, 2 * hd + i - core * (hd - own)

    def early_set(i):
        return own + i + hold * (hd - own), own + i + hold * (2 * hd - own)

    def late_set(i):
        x, y = pair_set(i)
        return x + hold * (own + i - x), y + hold * (own + i - y)

    opening = seg == 0
    first_pair = jnp.logical_and(opening, prev_far)

    @pl.when(first_pair)
    def _():
        for i in range(own):
            pair_wait(i)
            fast_grads(0, i, [early_set(i)], keep)

    for n in range(own, hd):
        attend(n)

    @pl.when(jnp.logical_and(opening, jnp.logical_not(prev_far)))
    def _():
        for i in range(own):
            fast_grads(0, i, [early_set(i)], keep)
            pair_wait(i)

    for s in range(GROUPS):
        @pl.when(seg == s)
        def _(s=s):
            for i in range(own):
                if s == 0:
                    fast_grads(s, i, [late_set(i)], share_late)
                else:
                    pair_wait(i)
                    fast_grads(s, i, [(own + i, own + i), pair_set(i)], share)
            if s == 0:
                @pl.when(is_last)
                def _():
                    for m in ORDER:
                        for i in range(own):
                            mate_start(i, m)

                @pl.when(jnp.logical_not(is_last))
                def _():
                    for m in ORDER:
                        for i in range(own):
                            tot[i, m] = with_mates(i, m, tot[i, m])
            else:
                for m in ORDER:
                    for i in range(own):
                        tot[i, m] = with_mates(i, m, tot[i, m])

        if s == 0:
            @pl.when(seg > 0)
            def _():
                for m in ORDER:
                    for i in range(own):
                        relay(i, m).wait_recv()
                        for c in range(2):
                            if m in relayed(c):
                                @pl.when(relays[c])
                                def _(i=i, m=m):
                                    relay(i, m).start()

                        tot[i, m] = fw[i, m].astype(F32)

        @pl.when(seg >= s)
        def _(s=s):
            for i in range(own):
                rate = step_ref[core * own + i]
                ortho = newton_schulz([tot[i, m] for m in range(3)])
                for m in range(3):
                    moved = wf[i, m] - rate * ortho[m]
                    w = moved * (target[i, m] / (lengths(moved, AXES[m]) + 1e-06))
                    high, low = split(w)
                    wo[i, m] = high
                    if s < GROUPS - 1:
                        wf[i, m] = w
                        wb[s + 1, i, m] = side(high, low)

            @pl.when(seg == s)
            def _():
                for i in range(own):
                    for m in range(3):
                        w_copy(i, m).start()

    ones = jnp.ones((8, dh), BF)
    sums = jnp.zeros((8, rows), F32)
    for n in [*range(own, hd), *range(own)]:
        if n < own:
            for m in range(3):
                w_copy(n, m).wait_recv()
        final = wr if n < own else wo
        i = n if n < own else n - own
        x = qn[n]
        gate = dot_nt(x, final[i, 0])
        upward = dot_nt(x, final[i, 1])
        hidden = (gate * sigmoid(gate) * upward).astype(BF)
        out = dot_nn(hidden, final[i, 2])
        fast = (out * scale_ref[head_of(n, core)]).astype(BF)
        both = att[n].astype(F32) + fast.astype(F32)
        comb[n] = both
        high, low = split(both * both)
        sums = sums + dot_nt(side(ones, ones), side(high, low))
    sums = jnp.maximum(sums, 0.0)
    part[...] = sums[:1]

    def head_copy(step):
        return pltpu.make_async_remote_copy(
            src_ref=part,
            dst_ref=others.at[step - 1],
            send_sem=head_send.at[step - 1],
            recv_sem=head_recv.at[step - 1],
            device_id=(p, head_at(step)),
            device_id_type=MESH,
        )

    for step in range(1, nh):
        head_copy(step).start()
    total = sums[:1]
    for step in range(1, nh):
        head_copy(step).wait_recv()
        total = total + others[step - 1]
    total = jnp.broadcast_to(total, (8, rows))
    high, low = split(lax.rsqrt(total / (width * nh) + 1e-05))
    eighths = jnp.full((16, dh), 0.125, BF)
    inverse = dot_tn(over(high.astype(F32), low.astype(F32)).astype(BF), eighths)
    for n in range(hd):
        out_ref[:, cols_of(head_of(n, core))] = comb[n] * inverse

    for step in range(1, nh):
        head_copy(step).wait_send()

    @pl.when(has_next)
    def _():
        for n in range(hd):
            for which in range(2):
                kv_copy(n, which).wait_send()

    @pl.when(core == 1)
    def _():
        for i in range(own):
            y_copy(i).wait_send()

    for i in range(own):
        att_copy(i).wait_send()
        for m in range(3):
            w_copy(i, m).wait_send()
            for step in range(1, mates):
                mate_copy(step, i, m).wait_send()
    for c in range(2):
        @pl.when(jnp.logical_and(closes, core == c))
        def _(c=c):
            for m in ORDER:
                for at in fw_sends(c, m):
                    fw_direct(*at).wait_send()

        @pl.when(jnp.logical_and(seg > 0, relays[c]))
        def _(c=c):
            for i in range(own):
                for m in relayed(c):
                    relay(i, m).wait_send()


def shards(
    queries, key_rows, values, gate_init, up_init, down_init, step_size, head_scale, out_gain
):
    rows, width = queries.shape
    hd, dh, fwh = gate_init.shape
    frames, nh = lax.axis_size("frame"), lax.axis_size("head")
    mates = frames // GROUPS // 2
    own = hd // 2
    dma = pltpu.SemaphoreType.DMA
    vmem = pl.BlockSpec(memory_space=pltpu.VMEM)
    scaled = pl.pallas_call(
        functools.partial(kernel, (frames, nh, hd)),
        out_shape=pltpu.VMEM((rows, width), F32),
        in_specs=[pl.BlockSpec(memory_space=pl.ANY)] * 8,
        out_specs=vmem,
        scratch_shapes=[
            pltpu.VMEM((hd, rows, dh), BF),
            pltpu.VMEM((hd, rows, dh), BF),
            pltpu.VMEM((2 * hd + own, rows, dh), BF),
            pltpu.VMEM((own, dh, fwh), F32),
            pltpu.VMEM((own, dh, fwh), F32),
            pltpu.VMEM((own, fwh, dh), F32),
            pltpu.SMEM((hd,), F32),
            pltpu.SMEM((hd,), F32),
            dma((3 * hd + 5,)),
            pltpu.VMEM((hd, rows, dh), BF),
            pltpu.VMEM((hd, rows, rows), F32),
            pltpu.VMEM((hd, rows, rows), BF),
            pltpu.VMEM((hd, rows, dh), F32),
            pltpu.VMEM((hd, rows, 1), F32),
            pltpu.VMEM((hd, rows, 1), F32),
            pltpu.VMEM((hd + own, rows, dh), BF),
            pltpu.VMEM((hd, rows, dh), BF),
            pltpu.VMEM((hd, rows, dh), F32),
            pltpu.VMEM((GROUPS, own, 3, dh, 2 * fwh), BF),
            pltpu.VMEM((own, 3, dh, fwh), F32),
            pltpu.VMEM((own, 3, dh, fwh), F32),
            pltpu.VMEM((own, 3, dh, fwh), F32),
            pltpu.VMEM((2, 2, fwh, rows), F32),
            pltpu.VMEM((2, fwh, rows), BF),
            pltpu.VMEM((2 * own, 3, dh, fwh), SENT),
            pltpu.VMEM((max(mates - 1, 1), own, 3, dh, fwh), SENT),
            pltpu.VMEM((own, 3, dh, fwh), F32),
            pltpu.VMEM((own, 3, dh, fwh), SENT),
            pltpu.VMEM((own, 3, dh, fwh), BF),
            pltpu.VMEM((own, 3, dh, fwh), BF),
            pltpu.VMEM((1, rows), F32),
            pltpu.VMEM((max(nh - 1, 1), 1, rows), F32),
            pltpu.SemaphoreType.REGULAR((max(mates.bit_length(), 1),)),
            pltpu.SemaphoreType.REGULAR((max(nh.bit_length(), 1),)),
            dma((2 * hd,)), dma((2 * hd,)),
            dma((own,)), dma((own,)),
            dma((own,)), dma((own,)),
            dma((max(mates - 1, 1), own * 3)), dma((max(mates - 1, 1), own * 3)),
            dma((mates, own * 3)), dma((own * 3,)),
            dma((own * 3,)), dma((own * 3,)),
            dma((max(nh - 1, 1),)), dma((max(nh - 1, 1),)),
        ],
        compiler_params=pltpu.CompilerParams(
            collective_id=0, has_side_effects=True, vmem_limit_bytes=56 * 1024 * 1024
        ),
    )(
        queries, key_rows, values, gate_init, up_init, down_init, step_size, head_scale,
    )
    return (scaled * out_gain[None, :]).astype(BF)


def solution(mesh):
    in_specs = (
        P("frame", "head"),
        P("frame", "head"),
        P("frame", "head"),
        P("head", None, None),
        P("head", None, None),
        P("head", None, None),
        P("head"),
        P("head"),
        P("head"),
    )
    return jax.shard_map(
        shards, mesh=mesh, in_specs=in_specs, out_specs=P("frame", "head"), check_vma=False
    )
```

```python
import functools
import math

import jax
import jax.numpy as jnp
from jax import lax
from jax.experimental import pallas as pl
from jax.experimental.pallas import tpu as pltpu
from jax.sharding import PartitionSpec as P

NS_ITERS = 5
GROUPS = 2
MESH = pl.DeviceIdType.MESH
SENT = jnp.bfloat16
COARSE = 2
BF = jnp.bfloat16
F32 = jnp.float32
quintic_terms = (3.4445, -4.775, 2.0315)


def dot_nt(a, b):
    return lax.dot_general(a, b, (((1,), (1,)), ((), ())), preferred_element_type=F32)


def dot_nn(a, b):
    return lax.dot_general(a, b, (((1,), (0,)), ((), ())), preferred_element_type=F32)


def dot_tn(a, b):
    return lax.dot_general(a, b, (((0,), (0,)), ((), ())), preferred_element_type=F32)


def split(x):
    high = x.astype(BF)
    return high, (x - high.astype(F32)).astype(BF)


def side(*parts):
    return jnp.concatenate(parts, axis=1)


def over(*parts):
    return jnp.concatenate(parts, axis=0)


def sigmoid(v):
    return 0.5 * (1.0 + jnp.tanh(0.5 * v))


def parts_of(x, fine):
    return split(x) if fine else (x.astype(BF),)


def left(parts):
    return side(parts[0], parts[1], parts[0]) if len(parts) == 2 else parts[0]


def right(parts, axis):
    if len(parts) == 1:
        return parts[0]
    return jnp.concatenate((parts[0], parts[0], parts[1]), axis=axis)


def newton_schulz(grads):
    xs = []
    for m in grads:
        norm = jnp.sqrt(jnp.sum(m * m, keepdims=True))
        xs.append(m * (1.0 / (norm + 1e-07)))
    for step in range(NS_ITERS):
        fine = step >= COARSE
        halves = [parts_of(x, fine) for x in xs]
        squares = [dot_nt(left(h), right(h, 1)) for h in halves]
        sq = [parts_of(a, fine) for a in squares]
        quartics = [dot_nn(left(a), right(a, 0)) for a in sq]
        mixing = [quintic_terms[1] * a + quintic_terms[2] * q for a, q in zip(squares, quartics)]
        xs = [
            quintic_terms[0] * x + dot_nn(left(parts_of(b, fine)), right(h, 0))
            for x, b, h in zip(xs, mixing, halves)
        ]
    return xs


def lengths(m, axis):
    return jnp.sqrt(jnp.sum(m * m, axis=axis, keepdims=True))


AXES = (1, 1, 0)
ORDER = (2, 0, 1)


def kernel(
    dims,
    q_any, k_any, v_any, gate_any, up_any, down_any, step_any, scale_any,
    out_ref,
    qs, ks, vs, w_ref, step_ref, scale_ref, local_sem,
    kp, here, before, mix, top, den, att, qn, comb, wb, wf, target, gp, hid, backs, cs, rz, tot, fw, by, wo, wr, part, others, frame_sem, head_sem, by_send, by_recv,
    kv_send, kv_recv, y_send, y_recv, att_send, att_recv, mate_send, mate_recv, fw_send, fw_recv,
    w_send, w_recv, head_send, head_recv,
):
    frames, nh, hd = dims
    rows, width = q_any.shape
    dh = width // hd
    half = frames // GROUPS
    mates = half // 2
    own = hd // 2
    p = lax.axis_index("frame")
    j = lax.axis_index("head")
    core = lax.rem(p, 2)
    seg = p // half
    rank = lax.rem(p, half) // 2
    pair = p + 1 - 2 * core
    has_prev = p > 0
    has_next = p < frames - 1
    prev_far = jnp.logical_and(core == 0, has_prev)
    next_far = jnp.logical_and(core == 1, has_next)

    def head_of(n, c):
        return (1 - c) * own + n if n < own else c * own + n - own

    def cols_of(h):
        return pl.ds(pl.multiple_of(h * dh, dh), dh)

    mine = pl.ds(core * own, own)
    locals_ = []
    for at, (src, dst) in enumerate(((k_any, ks), (q_any, qs), (v_any, vs))):
        for n in range(hd):
            cols = cols_of(head_of(n, core))
            locals_.append(pltpu.make_async_copy(src.at[:, cols], dst.at[n], local_sem.at[at]))
    for m, src in enumerate((gate_any, up_any, down_any)):
        locals_.append(pltpu.make_async_copy(src.at[mine], w_ref.at[m], local_sem.at[3]))
    locals_.append(pltpu.make_async_copy(step_any, step_ref, local_sem.at[4]))
    locals_.append(pltpu.make_async_copy(scale_any, scale_ref, local_sem.at[5]))

    def settle(ref, sem):
        pltpu.make_async_copy(ref, ref, sem).wait()

    barrier = pltpu.get_barrier_semaphore()

    def signal(sem, frame_at, head_at):
        pl.semaphore_signal(sem, inc=1, device_id=(frame_at, head_at), device_id_type=MESH)

    def mate_at(step):
        return seg * half + 2 * lax.rem(rank + step, mates) + core

    def head_at(step):
        return lax.rem(j + step, nh)

    def flip(bit):
        return j + bit - 2 * bit * lax.rem(j // bit, 2)

    is_last = rank == mates - 1
    paired = nh & (nh - 1) == 0
    bits = [1 << k for k in range(nh.bit_length() - 1)]
    partners = [flip(bit) for bit in bits] if paired else [head_at(step) for step in range(1, nh)]

    def ring_signal(sem, reach):
        @pl.when(p + reach < frames)
        def _():
            signal(sem, p + reach, j)

        @pl.when(p >= reach)
        def _():
            signal(sem, p - reach, j)

    def ring_count(reach):
        return (p + reach < frames).astype(jnp.int32) + (p >= reach).astype(jnp.int32)

    signal(barrier, pair, j)

    @pl.when(next_far)
    def _():
        signal(barrier, p + 1, j)

    @pl.when(prev_far)
    def _():
        signal(barrier, p - 1, j)

    ring_signal(barrier, 2)
    for to in partners:
        signal(barrier, p, to)
    for copy in locals_:
        copy.start()
    far = prev_far.astype(jnp.int32) + next_far.astype(jnp.int32)
    pl.semaphore_wait(barrier, 1 + far + ring_count(2) + len(partners))

    frame_rounds = max((mates - 1).bit_length(), 0)
    head_rounds = len(bits) - 1 if paired else 0

    def frame_signal(k):
        ring_signal(frame_sem.at[k], 2 << k)

    def head_signal(k):
        for to in partners:
            signal(head_sem.at[k], p, to)

    def rounds():
        for k in range(frame_rounds):
            pl.semaphore_wait(frame_sem.at[k], ring_count(2 << k))
            if k + 1 < frame_rounds:
                frame_signal(k + 1)
        for k in range(head_rounds):
            pl.semaphore_wait(head_sem.at[k], len(partners))
            if k + 1 < head_rounds:
                head_signal(k + 1)

    ahead = jnp.minimum(p + 1, frames - 1)

    def kv_copy(n, which):
        cols = cols_of(head_of(n, 1 - core))
        src, dst = ((k_any, kp.at[n]), (v_any, vs.at[hd + n]))[which]
        return pltpu.make_async_remote_copy(
            src_ref=src.at[:, cols],
            dst_ref=dst,
            send_sem=kv_send,
            recv_sem=kv_recv.at[2 * n + which],
            device_id=(ahead, j),
            device_id_type=MESH,
        )

    def y_copy(i):
        return pltpu.make_async_remote_copy(
            src_ref=v_any.at[:, pl.ds(i * dh, dh)],
            dst_ref=vs.at[2 * hd + i],
            send_sem=y_send.at[i],
            recv_sem=y_recv.at[i],
            device_id=(pair, j),
            device_id_type=MESH,
        )

    def att_copy(i):
        return pltpu.make_async_remote_copy(
            src_ref=att.at[i],
            dst_ref=att.at[hd + i],
            send_sem=att_send.at[i],
            recv_sem=att_recv.at[i],
            device_id=(pair, j),
            device_id_type=MESH,
        )

    @pl.when(has_next)
    def _():
        for which in range(2):
            for n in range(hd):
                kv_copy(n, which).start()

    @pl.when(core == 1)
    def _():
        for i in range(own):
            y_copy(i).start()

    if frame_rounds:
        frame_signal(0)
    if head_rounds:
        head_signal(0)

    factor = math.log2(math.e) / math.sqrt(dh)

    block = min(rows, 256)

    settle(ks, local_sem.at[0])
    settle(qs, local_sem.at[1])
    settle(vs.at[pl.ds(0, hd)], local_sem.at[2])
    settle(w_ref, local_sem.at[3])
    for copy in locals_[-2:]:
        copy.wait()

    def exps(q, keys):
        scores = dot_nt(q, keys) * factor
        high = jnp.max(scores, axis=1, keepdims=True)
        e = jnp.exp2(scores - high)
        return e, high, jnp.sum(e, axis=1, keepdims=True)

    for n in range(hd):
        for r in range(0, rows, block):
            rs = slice(r, r + block)
            e, t, d = exps(qs[n, rs], ks[n])
            here[n, rs] = e
            top[n, rs] = t
            den[n, rs] = d
        qf = qs[n].astype(F32)
        mean = jnp.mean(qf * qf, axis=1, keepdims=True)
        qn[n] = (qf * lax.rsqrt(mean + 1e-06)).astype(BF)
    for i in range(own):
        for m in range(3):
            w = w_ref[m, i]
            w = w.T if AXES[m] else w
            wf[i, m] = w
            target[i, m] = jnp.broadcast_to(lengths(w, AXES[m]), w.shape)
            high, low = split(w)
            wb[0, i, m] = side(high, low)

    def weigh(n):
        @pl.when(has_prev)
        def _():
            kv_copy(n, 0).wait_recv()
            for r in range(0, rows, block):
                rs = slice(r, r + block)
                e, t, d = exps(qs[n, rs], kp[n])
                t0 = top[n, rs]
                high = jnp.maximum(t, t0)
                a, b = jnp.exp2(t0 - high), jnp.exp2(t - high)
                inv = 1.0 / (den[n, rs] * a + d * b)
                before[n, rs] = (e * (b * inv)).astype(BF)
                probs = (here[n, rs] * (a * inv)).astype(BF)
                mix[n, rs] = dot_nn(probs, vs[n])

        @pl.when(jnp.logical_not(has_prev))
        def _():
            for r in range(0, rows, block):
                rs = slice(r, r + block)
                probs = (here[n, rs] * (1.0 / den[n, rs])).astype(BF)
                mix[n, rs] = dot_nn(probs, vs[n])

    def attend(n):
        @pl.when(has_prev)
        def _():
            kv_copy(n, 1).wait_recv()
            mix[n] = mix[n] + dot_nn(before[n], vs[hd + n])

        m = mix[n]
        mean = jnp.mean(m * m, axis=1, keepdims=True)
        att[n] = (m * lax.rsqrt(mean + 1e-06)).astype(BF)

    for n in range(hd):
        weigh(n)
    for n in range(own):
        attend(n)
        att_copy(n).start()
    rounds()

    def mate_copy(step, i, m):
        return pltpu.make_async_remote_copy(
            src_ref=cs.at[i, m],
            dst_ref=rz.at[step - 1, i, m],
            send_sem=mate_send.at[step - 1],
            recv_sem=mate_recv.at[step - 1, i * 3 + m],
            device_id=(mate_at(step), j),
            device_id_type=MESH,
        )

    beyond = jnp.minimum(p + 2, frames - 1)

    def fw_copy(src, frame_at, k, i, m):
        return pltpu.make_async_remote_copy(
            src_ref=src,
            dst_ref=fw.at[i, m],
            send_sem=fw_send.at[k],
            recv_sem=fw_recv.at[i * 3 + m],
            device_id=(frame_at, j),
            device_id_type=MESH,
        )

    def fw_direct(k, i, m):
        return fw_copy(cs.at[own + i, m], half + 2 * k + core, k, i, m)

    def relay(i, m):
        return fw_copy(fw.at[i, m], beyond, 0, i, m)

    def aside(i, m):
        return pltpu.make_async_remote_copy(
            src_ref=cs.at[own + i, m],
            dst_ref=by.at[i, m],
            send_sem=by_send,
            recv_sem=by_recv.at[i * 3 + m],
            device_id=(pair, j),
            device_id_type=MESH,
        )

    def behalf(k, i, m):
        return fw_copy(by.at[i, m], half + 2 * k, k, i, m)

    fars = list(reversed(range(1, mates)))

    def fw_sends(c, i, m):
        near = [fw_direct(0, i, m)]
        if c == 1:
            return near
        if m == ORDER[-1]:
            return [fw_direct(k, i, m) for k in fars] + near
        return near + [aside(i, m)]

    relays = jnp.logical_and(core == 1, p < frames - 2)
    closes = jnp.logical_and(seg == 0, is_last)

    def w_copy(i, m):
        return pltpu.make_async_remote_copy(
            src_ref=wo.at[i, m],
            dst_ref=wr.at[i, m],
            send_sem=w_send,
            recv_sem=w_recv,
            device_id=(pair, j),
            device_id_type=MESH,
        )

    always = p < frames

    def fast_grads(state, i, sets, finish):
        @pl.when(always)
        def _():
            total = None
            for k, (xi, yi) in enumerate(sets):
                x = att[xi]
                xx = side(x, x)
                gate = dot_nt(wb[state, i, 0], xx)
                upward = dot_nt(wb[state, i, 1], xx)
                sig = sigmoid(gate)
                active = gate * sig
                hid[k, 0] = active
                hid[k, 1] = upward * sig * (1.0 + gate * (1.0 - sig))
                d = dot_nn((active * upward).astype(BF), vs[yi])
                total = d if total is None else total + d
            finish(i, 2, -total)

        @pl.when(always)
        def _():
            total = None
            for k, (xi, yi) in enumerate(sets):
                y = vs[yi]
                back = -dot_nt(wb[state, i, 2], side(y, y))
                backs[k] = (back * hid[k, 0]).astype(BF)
                d = dot_nn((back * hid[k, 1]).astype(BF), att[xi])
                total = d if total is None else total + d
            finish(i, 0, total)

        @pl.when(always)
        def _():
            total = None
            for k, (xi, yi) in enumerate(sets):
                d = dot_nn(backs[k], att[xi])
                total = d if total is None else total + d
            finish(i, 1, total)

    def keep(i, m, value):
        gp[i, m] = value

    def mate_start(i, m):
        for step in range(1, mates):
            mate_copy(step, i, m).start()

    def with_mates(i, m, total):
        for step in range(1, mates):
            mate_copy(step, i, m).wait_recv()
            total = total + rz[step - 1, i, m].astype(F32)
        return total

    def share(i, m, value):
        tot[i, m] = value
        cs[i, m] = value.astype(SENT)
        mate_start(i, m)

    def share_late(i, m, value):
        value = value + gp[i, m]
        cs[i, m] = value.astype(SENT)
        tot[i, m] = value

        @pl.when(jnp.logical_not(is_last))
        def _():
            mate_start(i, m)

        @pl.when(is_last)
        def _():
            total = with_mates(i, m, tot[i, m])
            tot[i, m] = total
            cs[own + i, m] = total.astype(SENT)

        for c in range(2):
            @pl.when(jnp.logical_and(is_last, core == c))
            def _(c=c):
                for copy in fw_sends(c, i, m):
                    copy.start()

    def pair_wait(i):
        att_copy(i).wait_recv()

        @pl.when(core == 0)
        def _():
            y_copy(i).wait_recv()

    hold = prev_far.astype(jnp.int32)

    def pair_set(i):
        return hd + i, 2 * hd + i - core * (hd - own)

    def early_set(i):
        return own + i + hold * (hd - own), own + i + hold * (2 * hd - own)

    def late_set(i):
        x, y = pair_set(i)
        return x + hold * (own + i - x), y + hold * (own + i - y)

    opening = seg == 0
    first_pair = jnp.logical_and(opening, prev_far)

    @pl.when(first_pair)
    def _():
        for i in range(own):
            pair_wait(i)
            fast_grads(0, i, [early_set(i)], keep)

    for n in range(own, hd):
        attend(n)

    @pl.when(jnp.logical_and(opening, jnp.logical_not(prev_far)))
    def _():
        for i in range(own):
            fast_grads(0, i, [early_set(i)], keep)
            pair_wait(i)

    for s in range(GROUPS):
        @pl.when(seg == s)
        def _(s=s):
            for i in range(own):
                if s == 0:
                    fast_grads(s, i, [late_set(i)], share_late)
                else:
                    pair_wait(i)
                    fast_grads(s, i, [(own + i, own + i), pair_set(i)], share)
            if s == 0:
                @pl.when(jnp.logical_and(is_last, core == 1))
                def _():
                    for m in ORDER[:-1]:
                        for i in range(own):
                            aside(i, m).wait_recv()
                            for k in fars:
                                behalf(k, i, m).start()

                @pl.when(is_last)
                def _():
                    for m in ORDER:
                        for i in range(own):
                            mate_start(i, m)

                @pl.when(jnp.logical_not(is_last))
                def _():
                    for m in ORDER:
                        for i in range(own):
                            tot[i, m] = with_mates(i, m, tot[i, m])
            else:
                for m in ORDER:
                    for i in range(own):
                        tot[i, m] = with_mates(i, m, tot[i, m])

        if s == 0:
            @pl.when(seg > 0)
            def _():
                for m in ORDER:
                    for i in range(own):
                        relay(i, m).wait_recv()

                        @pl.when(relays)
                        def _(i=i, m=m):
                            relay(i, m).start()

                        tot[i, m] = fw[i, m].astype(F32)

        @pl.when(seg >= s)
        def _(s=s):
            for i in range(own):
                rate = step_ref[core * own + i]
                ortho = newton_schulz([tot[i, m] for m in range(3)])
                for m in range(3):
                    moved = wf[i, m] - rate * ortho[m]
                    w = moved * (target[i, m] / (lengths(moved, AXES[m]) + 1e-06))
                    high, low = split(w)
                    wo[i, m] = high
                    if s < GROUPS - 1:
                        wf[i, m] = w
                        wb[s + 1, i, m] = side(high, low)

            @pl.when(seg == s)
            def _():
                for i in range(own):
                    for m in range(3):
                        w_copy(i, m).start()

    ones = jnp.ones((8, dh), BF)
    sums = jnp.zeros((8, rows), F32)
    for n in [*range(own, hd), *range(own)]:
        if n == 0:
            settle(wr, w_recv)
        final = wr if n < own else wo
        i = n if n < own else n - own
        x = qn[n]
        gate = dot_nt(x, final[i, 0])
        upward = dot_nt(x, final[i, 1])
        hidden = (gate * sigmoid(gate) * upward).astype(BF)
        out = dot_nn(hidden, final[i, 2])
        fast = (out * scale_ref[head_of(n, core)]).astype(BF)
        both = att[n].astype(F32) + fast.astype(F32)
        comb[n] = both
        high, low = split(both * both)
        sums = sums + dot_nt(side(ones, ones), side(high, low))
    sums = jnp.maximum(sums, 0.0)
    part[...] = sums[:1]

    def head_copy(step):
        return pltpu.make_async_remote_copy(
            src_ref=part,
            dst_ref=others.at[step - 1],
            send_sem=head_send,
            recv_sem=head_recv,
            device_id=(p, head_at(step)),
            device_id_type=MESH,
        )

    for step in range(1, nh):
        head_copy(step).start()
    total = sums[:1]
    if nh > 1:
        settle(others, head_recv)
    for step in range(1, nh):
        total = total + others[step - 1]
    total = jnp.broadcast_to(total, (8, rows))
    high, low = split(lax.rsqrt(total / (width * nh) + 1e-05))
    eighths = jnp.full((16, dh), 0.125, BF)
    inverse = dot_tn(over(high.astype(F32), low.astype(F32)).astype(BF), eighths)
    for n in range(hd):
        out_ref[:, cols_of(head_of(n, core))] = comb[n] * inverse

    if nh > 1:
        settle(others, head_send)

    @pl.when(has_next)
    def _():
        settle(vs.at[pl.ds(0, 2 * hd)], kv_send)

    @pl.when(core == 1)
    def _():
        for i in range(own):
            y_copy(i).wait_send()

    for i in range(own):
        att_copy(i).wait_send()
    settle(wo, w_send)
    for step in range(1, mates):
        settle(cs.at[pl.ds(0, own)], mate_send.at[step - 1])
    for c in range(2):
        @pl.when(jnp.logical_and(closes, core == c))
        def _(c=c):
            settle(fw, fw_send.at[0])
            for k in fars:
                settle(fw.at[:, pl.ds(0, 1 + c)], fw_send.at[k])
            if c == 0:
                settle(fw.at[:, pl.ds(0, 2)], by_send)

    @pl.when(jnp.logical_and(seg > 0, relays))
    def _():
        settle(fw, fw_send.at[0])


def shards(
    queries, key_rows, values, gate_init, up_init, down_init, step_size, head_scale, out_gain
):
    rows, width = queries.shape
    hd, dh, fwh = gate_init.shape
    frames, nh = lax.axis_size("frame"), lax.axis_size("head")
    mates = frames // GROUPS // 2
    own = hd // 2
    dma = pltpu.SemaphoreType.DMA
    vmem = pl.BlockSpec(memory_space=pltpu.VMEM)
    scaled = pl.pallas_call(
        functools.partial(kernel, (frames, nh, hd)),
        out_shape=pltpu.VMEM((rows, width), F32),
        in_specs=[pl.BlockSpec(memory_space=pl.ANY)] * 8,
        out_specs=vmem,
        scratch_shapes=[
            pltpu.VMEM((hd, rows, dh), BF),
            pltpu.VMEM((hd, rows, dh), BF),
            pltpu.VMEM((2 * hd + own, rows, dh), BF),
            pltpu.VMEM((3, own, dh, fwh), F32),
            pltpu.SMEM((hd,), F32),
            pltpu.SMEM((hd,), F32),
            dma((6,)),
            pltpu.VMEM((hd, rows, dh), BF),
            pltpu.VMEM((hd, rows, rows), F32),
            pltpu.VMEM((hd, rows, rows), BF),
            pltpu.VMEM((hd, rows, dh), F32),
            pltpu.VMEM((hd, rows, 1), F32),
            pltpu.VMEM((hd, rows, 1), F32),
            pltpu.VMEM((hd + own, rows, dh), BF),
            pltpu.VMEM((hd, rows, dh), BF),
            pltpu.VMEM((hd, rows, dh), F32),
            pltpu.VMEM((GROUPS, own, 3, dh, 2 * fwh), BF),
            pltpu.VMEM((own, 3, dh, fwh), F32),
            pltpu.VMEM((own, 3, dh, fwh), F32),
            pltpu.VMEM((own, 3, dh, fwh), F32),
            pltpu.VMEM((2, 2, fwh, rows), F32),
            pltpu.VMEM((2, fwh, rows), BF),
            pltpu.VMEM((2 * own, 3, dh, fwh), SENT),
            pltpu.VMEM((max(mates - 1, 1), own, 3, dh, fwh), SENT),
            pltpu.VMEM((own, 3, dh, fwh), F32),
            pltpu.VMEM((own, 3, dh, fwh), SENT),
            pltpu.VMEM((own, 3, dh, fwh), SENT),
            pltpu.VMEM((own, 3, dh, fwh), BF),
            pltpu.VMEM((own, 3, dh, fwh), BF),
            pltpu.VMEM((1, rows), F32),
            pltpu.VMEM((max(nh - 1, 1), 1, rows), F32),
            pltpu.SemaphoreType.REGULAR((max((mates - 1).bit_length(), 1),)),
            pltpu.SemaphoreType.REGULAR((max(nh.bit_length() - 2, 1),)),
            dma(()), dma((own * 3,)),
            dma(()), dma((2 * hd,)),
            dma((own,)), dma((own,)),
            dma((own,)), dma((own,)),
            dma((max(mates - 1, 1),)), dma((max(mates - 1, 1), own * 3)),
            dma((mates,)), dma((own * 3,)),
            dma(()), dma(()),
            dma(()), dma(()),
        ],
        compiler_params=pltpu.CompilerParams(
            collective_id=0, has_side_effects=True, vmem_limit_bytes=56 * 1024 * 1024
        ),
    )(
        queries, key_rows, values, gate_init, up_init, down_init, step_size, head_scale,
    )
    return (scaled * out_gain[None, :]).astype(BF)


def solution(mesh):
    in_specs = (
        P("frame", "head"),
        P("frame", "head"),
        P("frame", "head"),
        P("head", None, None),
        P("head", None, None),
        P("head", None, None),
        P("head"),
        P("head"),
        P("head"),
    )
    return jax.shard_map(
        shards, mesh=mesh, in_specs=in_specs, out_specs=P("frame", "head"), check_vma=False
    )
```

```python
import functools
import math

import jax
import jax.numpy as jnp
from jax import lax
from jax.experimental import pallas as pl
from jax.experimental.pallas import tpu as pltpu
from jax.sharding import PartitionSpec as P

NS_ITERS = 5
GROUPS = 2
MESH = pl.DeviceIdType.MESH
SENT = jnp.bfloat16
COARSE = 2
BF = jnp.bfloat16
F32 = jnp.float32
quintic_terms = (3.4445, -4.775, 2.0315)


def dot_nt(a, b):
    return lax.dot_general(a, b, (((1,), (1,)), ((), ())), preferred_element_type=F32)


def dot_nn(a, b):
    return lax.dot_general(a, b, (((1,), (0,)), ((), ())), preferred_element_type=F32)


def dot_tn(a, b):
    return lax.dot_general(a, b, (((0,), (0,)), ((), ())), preferred_element_type=F32)


def split(x):
    high = x.astype(BF)
    return high, (x - high.astype(F32)).astype(BF)


def side(*parts):
    return jnp.concatenate(parts, axis=1)


def over(*parts):
    return jnp.concatenate(parts, axis=0)


def sigmoid(v):
    return 0.5 * (1.0 + jnp.tanh(0.5 * v))


def parts_of(x, fine):
    return split(x) if fine else (x.astype(BF),)


def left(parts):
    return side(parts[0], parts[1], parts[0]) if len(parts) == 2 else parts[0]


def right(parts, axis):
    if len(parts) == 1:
        return parts[0]
    return jnp.concatenate((parts[0], parts[0], parts[1]), axis=axis)


def newton_schulz(grads):
    scales = [1.0 / (jnp.sqrt(jnp.sum(m * m, keepdims=True)) + 1e-07) for m in grads]
    xs = [m * r for m, r in zip(grads, scales)]
    for step in range(NS_ITERS):
        fine = step >= COARSE
        halves = [parts_of(x, fine) for x in xs]
        if step == 0 and not fine:
            raw = [m.astype(BF) for m in grads]
            squares = [dot_nt(m, m) * (r * r) for m, r in zip(raw, scales)]
        else:
            squares = [dot_nt(left(h), right(h, 1)) for h in halves]
        sq = [parts_of(a, fine) for a in squares]
        quartics = [dot_nn(left(a), right(a, 0)) for a in sq]
        mixing = [quintic_terms[1] * a + quintic_terms[2] * q for a, q in zip(squares, quartics)]
        xs = [
            quintic_terms[0] * x + dot_nn(left(parts_of(b, fine)), right(h, 0))
            for x, b, h in zip(xs, mixing, halves)
        ]
    return xs


def lengths(m, axis):
    return jnp.sqrt(jnp.sum(m * m, axis=axis, keepdims=True))


AXES = (1, 1, 0)
ORDER = (2, 0, 1)


def kernel(
    dims,
    q_any, k_any, v_any, gate_any, up_any, down_any, step_any, scale_any,
    out_ref,
    qs, ks, vs, w_ref, step_ref, scale_ref, local_sem,
    kp, here, before, mix, top, den, att, qn, comb, wb, wf, target, gp, hid, backs, cs, rz, tot, fw, by, wo, fast, got, part, others, frame_sem, head_sem, pair_sem, out_send, qn_recv, by_send, by_recv,
    kv_send, kv_recv, y_send, y_recv, att_recv, mate_send, mate_recv, fw_send, fw_recv,
    fast_recv, head_send, head_recv,
):
    frames, nh, hd = dims
    rows, width = q_any.shape
    dh = width // hd
    half = frames // GROUPS
    mates = half // 2
    own = hd // 2
    p = lax.axis_index("frame")
    j = lax.axis_index("head")
    core = lax.rem(p, 2)
    seg = p // half
    rank = lax.rem(p, half) // 2
    pair = p + 1 - 2 * core
    has_prev = p > 0
    has_next = p < frames - 1
    prev_far = jnp.logical_and(core == 0, has_prev)
    next_far = jnp.logical_and(core == 1, has_next)

    def head_of(n, c):
        return (1 - c) * own + n if n < own else c * own + n - own

    def cols_of(h):
        return pl.ds(pl.multiple_of(h * dh, dh), dh)

    mine = pl.ds(core * own, own)
    locals_ = []
    for at, (src, dst) in enumerate(((k_any, ks), (q_any, qs), (v_any, vs))):
        for n in range(hd):
            cols = cols_of(head_of(n, core))
            locals_.append(pltpu.make_async_copy(src.at[:, cols], dst.at[n], local_sem.at[at]))
    for m, src in enumerate((gate_any, up_any, down_any)):
        locals_.append(pltpu.make_async_copy(src.at[mine], w_ref.at[m], local_sem.at[3]))
    locals_.append(pltpu.make_async_copy(step_any, step_ref, local_sem.at[4]))
    locals_.append(pltpu.make_async_copy(scale_any, scale_ref, local_sem.at[5]))

    def settle(ref, sem):
        pltpu.make_async_copy(ref, ref, sem).wait()

    barrier = pltpu.get_barrier_semaphore()

    def signal(sem, frame_at, head_at):
        pl.semaphore_signal(sem, inc=1, device_id=(frame_at, head_at), device_id_type=MESH)

    def mate_at(step):
        return seg * half + 2 * lax.rem(rank + step, mates) + core

    def head_at(step):
        return lax.rem(j + step, nh)

    def flip(bit):
        return j + bit - 2 * bit * lax.rem(j // bit, 2)

    def across(step):
        if not paired:
            return head_at(step)
        return j + sum((bit - 2 * bit * lax.rem(j // bit, 2)) for bit in bits if step & bit)

    is_last = rank == mates - 1
    paired = nh & (nh - 1) == 0
    bits = [1 << k for k in range(nh.bit_length() - 1)]
    partners = [flip(bit) for bit in bits] if paired else [head_at(step) for step in range(1, nh)]

    def ring_signal(sem, reach):
        @pl.when(p + reach < frames)
        def _():
            signal(sem, p + reach, j)

        @pl.when(p >= reach)
        def _():
            signal(sem, p - reach, j)

    def ring_count(reach):
        return (p + reach < frames).astype(jnp.int32) + (p >= reach).astype(jnp.int32)

    signal(barrier, pair, j)

    @pl.when(next_far)
    def _():
        signal(barrier, p + 1, j)

    @pl.when(prev_far)
    def _():
        signal(barrier, p - 1, j)

    ring_signal(barrier, 2)
    for to in partners:
        signal(barrier, p, to)
    for copy in locals_:
        copy.start()
    far = prev_far.astype(jnp.int32) + next_far.astype(jnp.int32)
    pl.semaphore_wait(barrier, 1 + far + ring_count(2) + len(partners))

    frame_rounds = max((mates - 1).bit_length(), 0)
    head_rounds = len(bits) - 1 if paired else 0

    def frame_signal(k):
        ring_signal(frame_sem.at[k], 2 << k)

    def head_signal(k):
        for to in partners:
            signal(head_sem.at[k], p, to)

    def rounds():
        for k in range(frame_rounds):
            pl.semaphore_wait(frame_sem.at[k], ring_count(2 << k))
            if k + 1 < frame_rounds:
                frame_signal(k + 1)
        for k in range(head_rounds):
            pl.semaphore_wait(head_sem.at[k], len(partners))
            if k + 1 < head_rounds:
                head_signal(k + 1)

    ahead = jnp.minimum(p + 1, frames - 1)

    def kv_copy(n, which):
        cols = cols_of(head_of(n, 1 - core))
        src, dst = ((k_any, kp.at[n]), (v_any, vs.at[hd + n]))[which]
        return pltpu.make_async_remote_copy(
            src_ref=src.at[:, cols],
            dst_ref=dst,
            send_sem=kv_send,
            recv_sem=kv_recv.at[2 * n + which],
            device_id=(ahead, j),
            device_id_type=MESH,
        )

    def y_copy(i):
        return pltpu.make_async_remote_copy(
            src_ref=v_any.at[:, pl.ds(i * dh, dh)],
            dst_ref=vs.at[2 * hd + i],
            send_sem=y_send.at[i],
            recv_sem=y_recv.at[i],
            device_id=(pair, j),
            device_id_type=MESH,
        )

    def qn_copy(i):
        return pltpu.make_async_remote_copy(
            src_ref=qn.at[i],
            dst_ref=qn.at[hd + i],
            send_sem=out_send,
            recv_sem=qn_recv,
            device_id=(pair, j),
            device_id_type=MESH,
        )

    def att_copy(i):
        return pltpu.make_async_remote_copy(
            src_ref=att.at[i],
            dst_ref=att.at[hd + i],
            send_sem=out_send,
            recv_sem=att_recv.at[i],
            device_id=(pair, j),
            device_id_type=MESH,
        )

    @pl.when(has_next)
    def _():
        for which in range(2):
            for n in range(hd):
                kv_copy(n, which).start()

    @pl.when(core == 1)
    def _():
        for i in range(own):
            y_copy(i).start()

    if frame_rounds:
        frame_signal(0)
    if head_rounds:
        head_signal(0)

    factor = math.log2(math.e) / math.sqrt(dh)

    block = min(rows, 256)

    settle(ks, local_sem.at[0])
    settle(qs, local_sem.at[1])
    settle(vs.at[pl.ds(0, hd)], local_sem.at[2])
    settle(w_ref, local_sem.at[3])
    for copy in locals_[-2:]:
        copy.wait()

    def exps(q, keys):
        scores = dot_nt(q, keys) * factor
        high = jnp.max(scores, axis=1, keepdims=True)
        e = jnp.exp2(scores - high)
        return e, high, jnp.sum(e, axis=1, keepdims=True)

    for n in range(hd):
        for r in range(0, rows, block):
            rs = slice(r, r + block)
            e, t, d = exps(qs[n, rs], ks[n])
            here[n, rs] = e
            top[n, rs] = t
            den[n, rs] = d
        qf = qs[n].astype(F32)
        mean = jnp.mean(qf * qf, axis=1, keepdims=True)
        qn[n] = (qf * lax.rsqrt(mean + 1e-06)).astype(BF)
    for i in range(own):
        qn_copy(i).start()
    for i in range(own):
        for m in range(3):
            w = w_ref[m, i]
            w = w.T if AXES[m] else w
            wf[i, m] = w
            target[i, m] = jnp.broadcast_to(lengths(w, AXES[m]), w.shape)
            high, low = split(w)
            wb[0, i, m] = side(high, low)

    def weigh(n):
        @pl.when(has_prev)
        def _():
            kv_copy(n, 0).wait_recv()
            for r in range(0, rows, block):
                rs = slice(r, r + block)
                e, t, d = exps(qs[n, rs], kp[n])
                t0 = top[n, rs]
                high = jnp.maximum(t, t0)
                a, b = jnp.exp2(t0 - high), jnp.exp2(t - high)
                inv = 1.0 / (den[n, rs] * a + d * b)
                before[n, rs] = (e * (b * inv)).astype(BF)
                probs = (here[n, rs] * (a * inv)).astype(BF)
                mix[n, rs] = dot_nn(probs, vs[n])

        @pl.when(jnp.logical_not(has_prev))
        def _():
            for r in range(0, rows, block):
                rs = slice(r, r + block)
                probs = (here[n, rs] * (1.0 / den[n, rs])).astype(BF)
                mix[n, rs] = dot_nn(probs, vs[n])

    def attend(n):
        @pl.when(has_prev)
        def _():
            kv_copy(n, 1).wait_recv()
            mix[n] = mix[n] + dot_nn(before[n], vs[hd + n])

        m = mix[n]
        mean = jnp.mean(m * m, axis=1, keepdims=True)
        att[n] = (m * lax.rsqrt(mean + 1e-06)).astype(BF)

    for n in range(hd):
        weigh(n)
    for n in range(own):
        attend(n)
        att_copy(n).start()
    rounds()
    signal(pair_sem, pair, j)

    def mate_copy(step, i, m):
        return pltpu.make_async_remote_copy(
            src_ref=cs.at[i, m],
            dst_ref=rz.at[step - 1, i, m],
            send_sem=mate_send.at[step - 1],
            recv_sem=mate_recv.at[step - 1, i * 3 + m],
            device_id=(mate_at(step), j),
            device_id_type=MESH,
        )

    beyond = jnp.minimum(p + 2, frames - 1)

    def fw_copy(src, frame_at, k, i, m):
        return pltpu.make_async_remote_copy(
            src_ref=src,
            dst_ref=fw.at[i, m],
            send_sem=fw_send.at[k],
            recv_sem=fw_recv.at[i * 3 + m],
            device_id=(frame_at, j),
            device_id_type=MESH,
        )

    def fw_direct(k, i, m):
        return fw_copy(cs.at[own + i, m], half + 2 * k + core, k, i, m)

    def relay(i, m):
        return fw_copy(fw.at[i, m], beyond, 0, i, m)

    def aside(i, m):
        return pltpu.make_async_remote_copy(
            src_ref=cs.at[own + i, m],
            dst_ref=by.at[i, m],
            send_sem=by_send,
            recv_sem=by_recv.at[i],
            device_id=(pair, j),
            device_id_type=MESH,
        )

    def behalf(k, i, m):
        return fw_copy(by.at[i, m], half + 2 * k, k, i, m)

    fars = list(reversed(range(1, mates)))

    def fw_sends(c, i, m):
        near = [fw_direct(0, i, m)]
        if c == 1:
            return near
        if m == ORDER[1]:
            return near + [aside(i, m)]
        far = [fw_direct(k, i, m) for k in fars]
        return near + far if m == ORDER[0] else far + near

    relays = jnp.logical_and(core == 1, p < frames - 2)

    always = p < frames

    def fast_grads(state, i, sets, finish):
        def join(ref, at):
            return ref[at[0]] if len(at) == 1 else over(*[ref[k] for k in at])

        xs, ys = [x for x, _ in sets], [y for _, y in sets]
        n = rows * len(sets)

        @pl.when(always)
        def _():
            x = join(att, xs)
            pre = dot_nt(over(wb[state, i, 0], wb[state, i, 1]), side(x, x))
            gate, upward = pre[:dh], pre[dh:]
            sig = sigmoid(gate)
            active = gate * sig
            hid[0, :, :n] = active
            hid[1, :, :n] = upward * sig * (1.0 + gate * (1.0 - sig))
            finish(i, 2, -dot_nn((active * upward).astype(BF), join(vs, ys)))

        @pl.when(always)
        def _():
            y = join(vs, ys)
            back = -dot_nt(wb[state, i, 2], side(y, y))
            backs[:, :n] = (back * hid[0, :, :n]).astype(BF)
            finish(i, 0, dot_nn((back * hid[1, :, :n]).astype(BF), join(att, xs)))

        @pl.when(always)
        def _():
            finish(i, 1, dot_nn(backs[:, :n], join(att, xs)))

    def keep(i, m, value):
        gp[i, m] = value

    def mate_start(i, m):
        for step in range(1, mates):
            mate_copy(step, i, m).start()

    def with_mates(i, m, total):
        for step in range(1, mates):
            mate_copy(step, i, m).wait_recv()
            total = total + rz[step - 1, i, m].astype(F32)
        return total

    def share(i, m, value):
        tot[i, m] = value
        cs[i, m] = value.astype(SENT)
        mate_start(i, m)

    def share_late(i, m, value):
        value = value + gp[i, m]
        cs[i, m] = value.astype(SENT)
        tot[i, m] = value

        @pl.when(jnp.logical_not(is_last))
        def _():
            mate_start(i, m)

        @pl.when(is_last)
        def _():
            total = with_mates(i, m, tot[i, m])
            tot[i, m] = total
            cs[own + i, m] = total.astype(SENT)

        for c in range(2):
            @pl.when(jnp.logical_and(is_last, core == c))
            def _(c=c):
                for copy in fw_sends(c, i, m):
                    copy.start()

    def pair_wait(i):
        att_copy(i).wait_recv()

        @pl.when(core == 0)
        def _():
            y_copy(i).wait_recv()

    hold = prev_far.astype(jnp.int32)

    def pair_set(i):
        return hd + i, 2 * hd + i - core * (hd - own)

    def early_set(i):
        return own + i + hold * (hd - own), own + i + hold * (2 * hd - own)

    def late_set(i):
        x, y = pair_set(i)
        return x + hold * (own + i - x), y + hold * (own + i - y)

    opening = seg == 0
    first_pair = jnp.logical_and(opening, prev_far)

    @pl.when(first_pair)
    def _():
        for i in range(own):
            pair_wait(i)
            fast_grads(0, i, [early_set(i)], keep)

    for n in range(own, hd):
        attend(n)

    @pl.when(jnp.logical_and(opening, jnp.logical_not(prev_far)))
    def _():
        for i in range(own):
            fast_grads(0, i, [early_set(i)], keep)
            pair_wait(i)

    for s in range(GROUPS):
        @pl.when(seg == s)
        def _(s=s):
            for i in range(own):
                if s == 0:
                    fast_grads(s, i, [late_set(i)], share_late)
                else:
                    pair_wait(i)
                    fast_grads(s, i, [(own + i, own + i), pair_set(i)], share)
            if s == 0:
                @pl.when(jnp.logical_and(is_last, core == 1))
                def _():
                    for i in range(own):
                        aside(i, ORDER[1]).wait_recv()
                        for k in fars:
                            behalf(k, i, ORDER[1]).start()

                for c in range(2):
                    @pl.when(jnp.logical_and(is_last, core == c))
                    def _(c=c):
                        settle(fw, fw_send.at[0])
                        for k in fars:
                            settle(fw.at[:, pl.ds(0, 2 - c)], fw_send.at[k])
                        if c == 0:
                            settle(fw.at[:, pl.ds(0, 1)], by_send)

                @pl.when(is_last)
                def _():
                    for m in ORDER:
                        for i in range(own):
                            mate_start(i, m)

                @pl.when(jnp.logical_not(is_last))
                def _():
                    for m in ORDER:
                        for i in range(own):
                            tot[i, m] = with_mates(i, m, tot[i, m])
            else:
                for m in ORDER:
                    for i in range(own):
                        tot[i, m] = with_mates(i, m, tot[i, m])

        if s == 0:
            @pl.when(seg > 0)
            def _():
                for m in ORDER:
                    for i in range(own):
                        relay(i, m).wait_recv()

                        @pl.when(relays)
                        def _(i=i, m=m):
                            relay(i, m).start()

                        tot[i, m] = fw[i, m].astype(F32)

        @pl.when(seg >= s)
        def _(s=s):
            for i in range(own):
                rate = step_ref[core * own + i]
                ortho = newton_schulz([tot[i, m] for m in range(3)])
                for m in range(3):
                    moved = wf[i, m] - rate * ortho[m]
                    w = moved * (target[i, m] / (lengths(moved, AXES[m]) + 1e-06))
                    high, low = split(w)
                    wo[i, m] = high
                    if s < GROUPS - 1:
                        wf[i, m] = w
                        wb[s + 1, i, m] = side(high, low)

    def fast_copy(t, i):
        return pltpu.make_async_remote_copy(
            src_ref=fast.at[t, i],
            dst_ref=got.at[i],
            send_sem=out_send,
            recv_sem=fast_recv,
            device_id=(pair, j),
            device_id_type=MESH,
        )

    def head_copy(t, step):
        return pltpu.make_async_remote_copy(
            src_ref=part.at[t],
            dst_ref=others.at[jnp.abs(core - t) * nh + step],
            send_sem=head_send,
            recv_sem=head_recv,
            device_id=(p - core + t, across(step)),
            device_id_type=MESH,
        )

    settle(qn.at[pl.ds(0, own)], qn_recv)
    pl.semaphore_wait(pair_sem, 1)
    ones = jnp.ones((8, dh), BF)
    sums = [jnp.zeros((8, rows), F32)] * 2
    for i in range(own):
        places = [own + i + jnp.abs(core - t) * (hd - own) for t in range(2)]
        x = over(*[qn[at] for at in places])
        gate = dot_nt(x, wo[i, 0])
        upward = dot_nt(x, wo[i, 1])
        hidden = (gate * sigmoid(gate) * upward).astype(BF)
        out = dot_nn(hidden, wo[i, 2])
        rounded = (out * scale_ref[core * own + i]).astype(BF)
        for t, at in enumerate(places):
            piece = rounded[t * rows:(t + 1) * rows]
            fast[t, i] = piece
            both = att[at].astype(F32) + piece.astype(F32)
            high, low = split(both * both)
            sums[t] = sums[t] + dot_nt(side(ones, ones), side(high, low))
    for t in range(2):
        part[t] = jnp.maximum(sums[t], 0.0)[:1]
    for t in range(2):
        for step in reversed(range(1, nh)):
            head_copy(t, step).start()

        @pl.when(core != t)
        def _(t=t):
            head_copy(t, 0).start()
            for i in range(own):
                fast_copy(t, i).start()

    for i in range(own):
        comb[own + i] = att[own + i].astype(F32) + fast[core, i].astype(F32)
    settle(got, fast_recv)
    for i in range(own):
        comb[i] = att[i].astype(F32) + got[i].astype(F32)
    settle(others.at[pl.ds(1, 2 * nh - 1)], head_recv)
    total = part[core]
    for at in range(1, 2 * nh):
        total = total + others[at]
    total = jnp.broadcast_to(total, (8, rows))
    high, low = split(lax.rsqrt(total / (width * nh) + 1e-05))
    eighths = jnp.full((16, dh), 0.125, BF)
    inverse = dot_tn(over(high.astype(F32), low.astype(F32)).astype(BF), eighths)
    for n in range(hd):
        out_ref[:, cols_of(head_of(n, core))] = comb[n] * inverse

    settle(others.at[pl.ds(1, 2 * nh - 1)], head_send)

    @pl.when(has_next)
    def _():
        settle(vs.at[pl.ds(0, 2 * hd)], kv_send)

    @pl.when(core == 1)
    def _():
        for i in range(own):
            y_copy(i).wait_send()

    sent = pl.ds(0, 3 * own)
    settle(vs.at[sent], out_send)
    for step in range(1, mates):
        settle(cs.at[pl.ds(0, own)], mate_send.at[step - 1])
    @pl.when(jnp.logical_and(seg > 0, relays))
    def _():
        settle(fw, fw_send.at[0])


def shards(
    queries, key_rows, values, gate_init, up_init, down_init, step_size, head_scale, out_gain
):
    rows, width = queries.shape
    hd, dh, fwh = gate_init.shape
    frames, nh = lax.axis_size("frame"), lax.axis_size("head")
    mates = frames // GROUPS // 2
    own = hd // 2
    dma = pltpu.SemaphoreType.DMA
    vmem = pl.BlockSpec(memory_space=pltpu.VMEM)
    scaled = pl.pallas_call(
        functools.partial(kernel, (frames, nh, hd)),
        out_shape=pltpu.VMEM((rows, width), F32),
        in_specs=[pl.BlockSpec(memory_space=pl.ANY)] * 8,
        out_specs=vmem,
        scratch_shapes=[
            pltpu.VMEM((hd, rows, dh), BF),
            pltpu.VMEM((hd, rows, dh), BF),
            pltpu.VMEM((2 * hd + own, rows, dh), BF),
            pltpu.VMEM((3, own, dh, fwh), F32),
            pltpu.SMEM((hd,), F32),
            pltpu.SMEM((hd,), F32),
            dma((6,)),
            pltpu.VMEM((hd, rows, dh), BF),
            pltpu.VMEM((hd, rows, rows), F32),
            pltpu.VMEM((hd, rows, rows), BF),
            pltpu.VMEM((hd, rows, dh), F32),
            pltpu.VMEM((hd, rows, 1), F32),
            pltpu.VMEM((hd, rows, 1), F32),
            pltpu.VMEM((hd + own, rows, dh), BF),
            pltpu.VMEM((hd + own, rows, dh), BF),
            pltpu.VMEM((hd, rows, dh), F32),
            pltpu.VMEM((GROUPS, own, 3, dh, 2 * fwh), BF),
            pltpu.VMEM((own, 3, dh, fwh), F32),
            pltpu.VMEM((own, 3, dh, fwh), F32),
            pltpu.VMEM((own, 3, dh, fwh), F32),
            pltpu.VMEM((2, fwh, 2 * rows), F32),
            pltpu.VMEM((fwh, 2 * rows), BF),
            pltpu.VMEM((2 * own, 3, dh, fwh), SENT),
            pltpu.VMEM((max(mates - 1, 1), own, 3, dh, fwh), SENT),
            pltpu.VMEM((own, 3, dh, fwh), F32),
            pltpu.VMEM((own, 3, dh, fwh), SENT),
            pltpu.VMEM((own, 3, dh, fwh), SENT),
            pltpu.VMEM((own, 3, dh, fwh), BF),
            pltpu.VMEM((2, own, rows, dh), BF),
            pltpu.VMEM((own, rows, dh), BF),
            pltpu.VMEM((2, 1, rows), F32),
            pltpu.VMEM((2 * nh, 1, rows), F32),
            pltpu.SemaphoreType.REGULAR((max((mates - 1).bit_length(), 1),)),
            pltpu.SemaphoreType.REGULAR((max(nh.bit_length() - 2, 1),)),
            pltpu.SemaphoreType.REGULAR,
            dma(()), dma(()),
            dma(()), dma((own,)),
            dma(()), dma((2 * hd,)),
            dma((own,)), dma((own,)),
            dma((own,)),
            dma((max(mates - 1, 1),)), dma((max(mates - 1, 1), own * 3)),
            dma((mates,)), dma((own * 3,)),
            dma(()),
            dma(()), dma(()),
        ],
        compiler_params=pltpu.CompilerParams(
            collective_id=0, has_side_effects=True, vmem_limit_bytes=56 * 1024 * 1024
        ),
    )(
        queries, key_rows, values, gate_init, up_init, down_init, step_size, head_scale,
    )
    return (scaled * out_gain[None, :]).astype(BF)


def solution(mesh):
    in_specs = (
        P("frame", "head"),
        P("frame", "head"),
        P("frame", "head"),
        P("head", None, None),
        P("head", None, None),
        P("head", None, None),
        P("head"),
        P("head"),
        P("head"),
    )
    return jax.shard_map(
        shards, mesh=mesh, in_specs=in_specs, out_specs=P("frame", "head"), check_vma=False
    )
```

```python
import functools
import math

import jax
import jax.numpy as jnp
from jax import lax
from jax.experimental import pallas as pl
from jax.experimental.pallas import tpu as pltpu
from jax.sharding import PartitionSpec as P

NS_ITERS = 5
GROUPS = 2
MESH = pl.DeviceIdType.MESH
SENT = jnp.bfloat16
COARSE = 2
BF = jnp.bfloat16
F32 = jnp.float32
quintic_terms = (3.4445, -4.775, 2.0315)


def dot_nt(a, b):
    return lax.dot_general(a, b, (((1,), (1,)), ((), ())), preferred_element_type=F32)


def dot_nn(a, b):
    return lax.dot_general(a, b, (((1,), (0,)), ((), ())), preferred_element_type=F32)


def dot_tn(a, b):
    return lax.dot_general(a, b, (((0,), (0,)), ((), ())), preferred_element_type=F32)


def split(x):
    high = x.astype(BF)
    return high, (x - high.astype(F32)).astype(BF)


def side(*parts):
    return jnp.concatenate(parts, axis=1)


def over(*parts):
    return jnp.concatenate(parts, axis=0)


def sigmoid(v):
    return 0.5 * (1.0 + jnp.tanh(0.5 * v))


def parts_of(x, fine):
    return split(x) if fine else (x.astype(BF),)


def left(parts):
    return side(parts[0], parts[1], parts[0]) if len(parts) == 2 else parts[0]


def right(parts, axis):
    if len(parts) == 1:
        return parts[0]
    return jnp.concatenate((parts[0], parts[0], parts[1]), axis=axis)


def newton_schulz(grads):
    scales = [1.0 / (jnp.sqrt(jnp.sum(m * m, keepdims=True)) + 1e-07) for m in grads]
    xs = [m * r for m, r in zip(grads, scales)]
    for step in range(NS_ITERS):
        fine = step >= COARSE
        halves = [parts_of(x, fine) for x in xs]
        if step == 0 and not fine:
            raw = [m.astype(BF) for m in grads]
            squares = [dot_nt(m, m) * (r * r) for m, r in zip(raw, scales)]
        else:
            squares = [dot_nt(left(h), right(h, 1)) for h in halves]
        sq = [parts_of(a, fine) for a in squares]
        quartics = [dot_nn(left(a), right(a, 0)) for a in sq]
        mixing = [quintic_terms[1] * a + quintic_terms[2] * q for a, q in zip(squares, quartics)]
        xs = [
            quintic_terms[0] * x + dot_nn(left(parts_of(b, fine)), right(h, 0))
            for x, b, h in zip(xs, mixing, halves)
        ]
    return xs


def lengths(m, axis):
    return jnp.sqrt(jnp.sum(m * m, axis=axis, keepdims=True))


AXES = (1, 1, 0)
ORDER = (2, 0, 1)


def kernel(
    dims,
    q_any, k_any, v_any, gate_any, up_any, down_any, step_any, scale_any,
    out_ref,
    qs, ks, vs, w_ref, step_ref, scale_ref, local_sem,
    kp, here, before, mix, top, den, att, qn, comb, wb, wf, target, gp, hid, backs, cs, rz, tot, fw, by, wo, fast, got, part, others, frame_sem, head_sem, pair_sem, out_send, qn_recv, by_send, by_recv,
    kv_send, kv_recv, y_send, y_recv, att_recv, mate_send, mate_recv, fw_send, fw_recv,
    fast_recv, head_send, head_recv,
):
    frames, nh, hd = dims
    rows, width = q_any.shape
    dh = width // hd
    half = frames // GROUPS
    mates = half // 2
    own = hd // 2
    p = lax.axis_index("frame")
    j = lax.axis_index("head")
    core = lax.rem(p, 2)
    seg = p // half
    rank = lax.rem(p, half) // 2
    pair = p + 1 - 2 * core
    has_prev = p > 0
    has_next = p < frames - 1
    prev_far = jnp.logical_and(core == 0, has_prev)
    next_far = jnp.logical_and(core == 1, has_next)

    def head_of(n, c):
        return (1 - c) * own + n if n < own else c * own + n - own

    def cols_of(h):
        return pl.ds(pl.multiple_of(h * dh, dh), dh)

    mine = pl.ds(core * own, own)
    locals_ = []
    for at, (src, dst) in enumerate(((k_any, ks), (q_any, qs), (v_any, vs))):
        for n in range(hd):
            cols = cols_of(head_of(n, core))
            locals_.append(pltpu.make_async_copy(src.at[:, cols], dst.at[n], local_sem.at[at]))
    for m, src in enumerate((gate_any, up_any, down_any)):
        locals_.append(pltpu.make_async_copy(src.at[mine], w_ref.at[m], local_sem.at[3]))
    locals_.append(pltpu.make_async_copy(step_any, step_ref, local_sem.at[4]))
    locals_.append(pltpu.make_async_copy(scale_any, scale_ref, local_sem.at[5]))

    def settle(ref, sem):
        pltpu.make_async_copy(ref, ref, sem).wait()

    barrier = pltpu.get_barrier_semaphore()

    def signal(sem, frame_at, head_at):
        pl.semaphore_signal(sem, inc=1, device_id=(frame_at, head_at), device_id_type=MESH)

    def mate_at(step):
        return seg * half + 2 * lax.rem(rank + step, mates) + core

    def head_at(step):
        return lax.rem(j + step, nh)

    def flip(bit):
        return j + bit - 2 * bit * lax.rem(j // bit, 2)

    def across(step):
        if not paired:
            return head_at(step)
        return j + sum((bit - 2 * bit * lax.rem(j // bit, 2)) for bit in bits if step & bit)

    is_last = rank == mates - 1
    paired = nh & (nh - 1) == 0
    bits = [1 << k for k in range(nh.bit_length() - 1)]
    partners = [flip(bit) for bit in bits] if paired else [head_at(step) for step in range(1, nh)]

    def ring_signal(sem, reach):
        @pl.when(p + reach < frames)
        def _():
            signal(sem, p + reach, j)

        @pl.when(p >= reach)
        def _():
            signal(sem, p - reach, j)

    def ring_count(reach):
        return (p + reach < frames).astype(jnp.int32) + (p >= reach).astype(jnp.int32)

    signal(barrier, pair, j)

    @pl.when(next_far)
    def _():
        signal(barrier, p + 1, j)

    @pl.when(prev_far)
    def _():
        signal(barrier, p - 1, j)

    ring_signal(barrier, 2)
    for to in partners:
        signal(barrier, p, to)
    for copy in locals_:
        copy.start()
    far = prev_far.astype(jnp.int32) + next_far.astype(jnp.int32)
    pl.semaphore_wait(barrier, 1 + far + ring_count(2) + len(partners))

    frame_rounds = max((mates - 1).bit_length(), 0)
    head_rounds = len(bits) - 1 if paired else 0

    def frame_signal(k):
        ring_signal(frame_sem.at[k], 2 << k)

    def head_signal(k):
        for to in partners:
            signal(head_sem.at[k], p, to)

    def rounds():
        for k in range(frame_rounds):
            pl.semaphore_wait(frame_sem.at[k], ring_count(2 << k))
            if k + 1 < frame_rounds:
                frame_signal(k + 1)
        for k in range(head_rounds):
            pl.semaphore_wait(head_sem.at[k], len(partners))
            if k + 1 < head_rounds:
                head_signal(k + 1)

    ahead = jnp.minimum(p + 1, frames - 1)

    def kv_copy(n, which):
        cols = cols_of(head_of(n, 1 - core))
        src, dst = ((k_any, kp.at[n]), (v_any, vs.at[hd + n]))[which]
        return pltpu.make_async_remote_copy(
            src_ref=src.at[:, cols],
            dst_ref=dst,
            send_sem=kv_send,
            recv_sem=kv_recv.at[2 * n + which],
            device_id=(ahead, j),
            device_id_type=MESH,
        )

    def y_copy(i):
        return pltpu.make_async_remote_copy(
            src_ref=v_any.at[:, pl.ds(i * dh, dh)],
            dst_ref=vs.at[2 * hd + i],
            send_sem=y_send.at[i],
            recv_sem=y_recv.at[i],
            device_id=(pair, j),
            device_id_type=MESH,
        )

    def qn_copy(i):
        return pltpu.make_async_remote_copy(
            src_ref=qn.at[i],
            dst_ref=qn.at[hd + i],
            send_sem=out_send,
            recv_sem=qn_recv,
            device_id=(pair, j),
            device_id_type=MESH,
        )

    def att_copy(i):
        return pltpu.make_async_remote_copy(
            src_ref=att.at[i],
            dst_ref=att.at[hd + i],
            send_sem=out_send,
            recv_sem=att_recv.at[i],
            device_id=(pair, j),
            device_id_type=MESH,
        )

    @pl.when(has_next)
    def _():
        for which in range(2):
            for n in range(hd):
                kv_copy(n, which).start()

    @pl.when(core == 1)
    def _():
        for i in range(own):
            y_copy(i).start()

    if frame_rounds:
        frame_signal(0)
    if head_rounds:
        head_signal(0)

    factor = math.log2(math.e) / math.sqrt(dh)

    block = min(rows, 256)

    settle(ks, local_sem.at[0])
    settle(qs, local_sem.at[1])
    settle(vs.at[pl.ds(0, hd)], local_sem.at[2])
    settle(w_ref, local_sem.at[3])
    for copy in locals_[-2:]:
        copy.wait()

    def exps(q, keys):
        scores = dot_nt(q, keys) * factor
        high = jnp.max(scores, axis=1, keepdims=True)
        e = jnp.exp2(scores - high)
        return e, high, jnp.sum(e, axis=1, keepdims=True)

    for n in range(hd):
        for r in range(0, rows, block):
            rs = slice(r, r + block)
            e, t, d = exps(qs[n, rs], ks[n])
            here[n, rs] = e
            top[n, rs] = t
            den[n, rs] = d
        qf = qs[n].astype(F32)
        mean = jnp.mean(qf * qf, axis=1, keepdims=True)
        qn[n] = (qf * lax.rsqrt(mean + 1e-06)).astype(BF)
    for i in range(own):
        qn_copy(i).start()
    for i in range(own):
        for m in range(3):
            w = w_ref[m, i]
            w = w.T if AXES[m] else w
            wf[i, m] = w
            target[i, m] = jnp.broadcast_to(lengths(w, AXES[m]), w.shape)
            high, low = split(w)
            wb[0, i, m] = side(high, low)

    def weigh(n):
        @pl.when(has_prev)
        def _():
            kv_copy(n, 0).wait_recv()
            for r in range(0, rows, block):
                rs = slice(r, r + block)
                e, t, d = exps(qs[n, rs], kp[n])
                t0 = top[n, rs]
                high = jnp.maximum(t, t0)
                a, b = jnp.exp2(t0 - high), jnp.exp2(t - high)
                inv = 1.0 / (den[n, rs] * a + d * b)
                before[n, rs] = (e * (b * inv)).astype(BF)
                probs = (here[n, rs] * (a * inv)).astype(BF)
                mix[n, rs] = dot_nn(probs, vs[n])

        @pl.when(jnp.logical_not(has_prev))
        def _():
            for r in range(0, rows, block):
                rs = slice(r, r + block)
                probs = (here[n, rs] * (1.0 / den[n, rs])).astype(BF)
                mix[n, rs] = dot_nn(probs, vs[n])

    def attend(n):
        @pl.when(has_prev)
        def _():
            kv_copy(n, 1).wait_recv()
            mix[n] = mix[n] + dot_nn(before[n], vs[hd + n])

        m = mix[n]
        mean = jnp.mean(m * m, axis=1, keepdims=True)
        att[n] = (m * lax.rsqrt(mean + 1e-06)).astype(BF)

    for n in range(hd):
        weigh(n)
    for n in range(own):
        attend(n)
        att_copy(n).start()
    rounds()
    signal(pair_sem, pair, j)

    def mate_copy(step, i, m):
        return pltpu.make_async_remote_copy(
            src_ref=cs.at[i, m],
            dst_ref=rz.at[step - 1, i, m],
            send_sem=mate_send.at[step - 1],
            recv_sem=mate_recv.at[step - 1, i * 3 + m],
            device_id=(mate_at(step), j),
            device_id_type=MESH,
        )

    beyond = jnp.minimum(p + 2, frames - 1)

    def fw_copy(src, frame_at, k, i, m):
        return pltpu.make_async_remote_copy(
            src_ref=src,
            dst_ref=fw.at[i, m],
            send_sem=fw_send.at[k],
            recv_sem=fw_recv.at[i * 3 + m],
            device_id=(frame_at, j),
            device_id_type=MESH,
        )

    def fw_direct(k, i, m):
        return fw_copy(cs.at[own + i, m], half + 2 * k + core, k, i, m)

    def relay(i, m):
        return fw_copy(fw.at[i, m], beyond, 0, i, m)

    def aside(i, m):
        return pltpu.make_async_remote_copy(
            src_ref=cs.at[own + i, m],
            dst_ref=by.at[i, m],
            send_sem=by_send,
            recv_sem=by_recv.at[i],
            device_id=(pair, j),
            device_id_type=MESH,
        )

    def behalf(k, i, m):
        return fw_copy(by.at[i, m], half + 2 * k, k, i, m)

    fars = list(reversed(range(1, mates)))

    def fw_sends(c, i, m):
        near = [fw_direct(0, i, m)]
        far = [fw_direct(k, i, m) for k in fars]
        if c == 1:
            return far + near if m == ORDER[-1] else near
        if m == ORDER[1]:
            return near + [aside(i, m)]
        return near + far if m == ORDER[0] else far + near

    relays = jnp.logical_and(core == 1, p < frames - 2)

    always = p < frames

    def fast_grads(state, i, sets, finish):
        def join(ref, at):
            return ref[at[0]] if len(at) == 1 else over(*[ref[k] for k in at])

        xs, ys = [x for x, _ in sets], [y for _, y in sets]
        n = rows * len(sets)

        @pl.when(always)
        def _():
            x = join(att, xs)
            pre = dot_nt(over(wb[state, i, 0], wb[state, i, 1]), side(x, x))
            gate, upward = pre[:dh], pre[dh:]
            sig = sigmoid(gate)
            active = gate * sig
            hid[0, :, :n] = active
            hid[1, :, :n] = upward * sig * (1.0 + gate * (1.0 - sig))
            finish(i, 2, -dot_nn((active * upward).astype(BF), join(vs, ys)))

        @pl.when(always)
        def _():
            y = join(vs, ys)
            back = -dot_nt(wb[state, i, 2], side(y, y))
            backs[:, :n] = (back * hid[0, :, :n]).astype(BF)
            finish(i, 0, dot_nn((back * hid[1, :, :n]).astype(BF), join(att, xs)))

        @pl.when(always)
        def _():
            finish(i, 1, dot_nn(backs[:, :n], join(att, xs)))

    def keep(i, m, value):
        gp[i, m] = value

    def mate_start(i, m):
        for step in range(1, mates):
            mate_copy(step, i, m).start()

    def with_mates(i, m, total):
        for step in range(1, mates):
            mate_copy(step, i, m).wait_recv()
            total = total + rz[step - 1, i, m].astype(F32)
        return total

    def share(i, m, value):
        tot[i, m] = value
        cs[i, m] = value.astype(SENT)
        mate_start(i, m)

    def share_late(i, m, value):
        value = value + gp[i, m]
        cs[i, m] = value.astype(SENT)
        tot[i, m] = value

        @pl.when(jnp.logical_not(is_last))
        def _():
            mate_start(i, m)

        @pl.when(is_last)
        def _():
            total = with_mates(i, m, tot[i, m])
            tot[i, m] = total
            cs[own + i, m] = total.astype(SENT)

        for c in range(2):
            @pl.when(jnp.logical_and(is_last, core == c))
            def _(c=c):
                for copy in fw_sends(c, i, m):
                    copy.start()

    def pair_wait(i):
        att_copy(i).wait_recv()

        @pl.when(core == 0)
        def _():
            y_copy(i).wait_recv()

    hold = prev_far.astype(jnp.int32)

    def pair_set(i):
        return hd + i, 2 * hd + i - core * (hd - own)

    def early_set(i):
        return own + i + hold * (hd - own), own + i + hold * (2 * hd - own)

    def late_set(i):
        x, y = pair_set(i)
        return x + hold * (own + i - x), y + hold * (own + i - y)

    opening = seg == 0
    first_pair = jnp.logical_and(opening, prev_far)

    @pl.when(first_pair)
    def _():
        for i in range(own):
            pair_wait(i)
            fast_grads(0, i, [early_set(i)], keep)

    for n in range(own, hd):
        attend(n)

    @pl.when(jnp.logical_and(opening, jnp.logical_not(prev_far)))
    def _():
        for i in range(own):
            fast_grads(0, i, [early_set(i)], keep)
            pair_wait(i)

    for s in range(GROUPS):
        @pl.when(seg == s)
        def _(s=s):
            for i in range(own):
                if s == 0:
                    fast_grads(s, i, [late_set(i)], share_late)
                else:
                    pair_wait(i)
                    fast_grads(s, i, [(own + i, own + i), pair_set(i)], share)
            if s == 0:
                @pl.when(jnp.logical_and(is_last, core == 1))
                def _():
                    for i in range(own):
                        aside(i, ORDER[1]).wait_recv()
                        for k in fars:
                            behalf(k, i, ORDER[1]).start()

                for c in range(2):
                    @pl.when(jnp.logical_and(is_last, core == c))
                    def _(c=c):
                        settle(fw, fw_send.at[0])
                        for k in fars:
                            settle(fw.at[:, pl.ds(0, 2)], fw_send.at[k])
                        if c == 0:
                            settle(fw.at[:, pl.ds(0, 1)], by_send)

                @pl.when(is_last)
                def _():
                    for m in ORDER:
                        for i in range(own):
                            mate_start(i, m)

                @pl.when(jnp.logical_not(is_last))
                def _():
                    for m in ORDER:
                        for i in range(own):
                            tot[i, m] = with_mates(i, m, tot[i, m])
            else:
                for m in ORDER:
                    for i in range(own):
                        tot[i, m] = with_mates(i, m, tot[i, m])

        if s == 0:
            @pl.when(seg > 0)
            def _():
                for m in ORDER:
                    for i in range(own):
                        relay(i, m).wait_recv()

                        if m != ORDER[-1]:
                            @pl.when(relays)
                            def _(i=i, m=m):
                                relay(i, m).start()

                        tot[i, m] = fw[i, m].astype(F32)

        @pl.when(seg >= s)
        def _(s=s):
            for i in range(own):
                rate = step_ref[core * own + i]
                ortho = newton_schulz([tot[i, m] for m in range(3)])
                for m in range(3):
                    moved = wf[i, m] - rate * ortho[m]
                    w = moved * (target[i, m] / (lengths(moved, AXES[m]) + 1e-06))
                    high, low = split(w)
                    wo[i, m] = high
                    if s < GROUPS - 1:
                        wf[i, m] = w
                        wb[s + 1, i, m] = side(high, low)

    def fast_copy(t, i):
        return pltpu.make_async_remote_copy(
            src_ref=fast.at[t, i],
            dst_ref=got.at[i],
            send_sem=out_send,
            recv_sem=fast_recv,
            device_id=(pair, j),
            device_id_type=MESH,
        )

    def head_copy(t, step):
        return pltpu.make_async_remote_copy(
            src_ref=part.at[t],
            dst_ref=others.at[jnp.abs(core - t) * nh + step],
            send_sem=head_send,
            recv_sem=head_recv,
            device_id=(p - core + t, across(step)),
            device_id_type=MESH,
        )

    settle(qn.at[pl.ds(0, own)], qn_recv)
    pl.semaphore_wait(pair_sem, 1)
    ones = jnp.ones((8, dh), BF)
    sums = [jnp.zeros((8, rows), F32)] * 2
    for i in range(own):
        places = [own + i + jnp.abs(core - t) * (hd - own) for t in range(2)]
        x = over(*[qn[at] for at in places])
        gate = dot_nt(x, wo[i, 0])
        upward = dot_nt(x, wo[i, 1])
        hidden = (gate * sigmoid(gate) * upward).astype(BF)
        out = dot_nn(hidden, wo[i, 2])
        rounded = (out * scale_ref[core * own + i]).astype(BF)
        for t, at in enumerate(places):
            piece = rounded[t * rows:(t + 1) * rows]
            fast[t, i] = piece
            both = att[at].astype(F32) + piece.astype(F32)
            high, low = split(both * both)
            sums[t] = sums[t] + dot_nt(side(ones, ones), side(high, low))
    for t in range(2):
        part[t] = jnp.maximum(sums[t], 0.0)[:1]
    for t in range(2):
        for step in reversed(range(1, nh)):
            head_copy(t, step).start()

        @pl.when(core != t)
        def _(t=t):
            head_copy(t, 0).start()
            for i in range(own):
                fast_copy(t, i).start()

    for i in range(own):
        comb[own + i] = att[own + i].astype(F32) + fast[core, i].astype(F32)
    settle(got, fast_recv)
    for i in range(own):
        comb[i] = att[i].astype(F32) + got[i].astype(F32)
    settle(others.at[pl.ds(1, 2 * nh - 1)], head_recv)
    total = part[core]
    for at in range(1, 2 * nh):
        total = total + others[at]
    total = jnp.broadcast_to(total, (8, rows))
    high, low = split(lax.rsqrt(total / (width * nh) + 1e-05))
    eighths = jnp.full((16, dh), 0.125, BF)
    inverse = dot_tn(over(high.astype(F32), low.astype(F32)).astype(BF), eighths)
    for n in range(hd):
        out_ref[:, cols_of(head_of(n, core))] = comb[n] * inverse

    settle(others.at[pl.ds(1, 2 * nh - 1)], head_send)

    @pl.when(has_next)
    def _():
        settle(vs.at[pl.ds(0, 2 * hd)], kv_send)

    @pl.when(core == 1)
    def _():
        for i in range(own):
            y_copy(i).wait_send()

    sent = pl.ds(0, 3 * own)
    settle(vs.at[sent], out_send)
    for step in range(1, mates):
        settle(cs.at[pl.ds(0, own)], mate_send.at[step - 1])
    @pl.when(jnp.logical_and(seg > 0, relays))
    def _():
        settle(fw.at[:, pl.ds(0, 2)], fw_send.at[0])


def shards(
    queries, key_rows, values, gate_init, up_init, down_init, step_size, head_scale, out_gain
):
    rows, width = queries.shape
    hd, dh, fwh = gate_init.shape
    frames, nh = lax.axis_size("frame"), lax.axis_size("head")
    mates = frames // GROUPS // 2
    own = hd // 2
    dma = pltpu.SemaphoreType.DMA
    vmem = pl.BlockSpec(memory_space=pltpu.VMEM)
    scaled = pl.pallas_call(
        functools.partial(kernel, (frames, nh, hd)),
        out_shape=pltpu.VMEM((rows, width), F32),
        in_specs=[pl.BlockSpec(memory_space=pl.ANY)] * 8,
        out_specs=vmem,
        scratch_shapes=[
            pltpu.VMEM((hd, rows, dh), BF),
            pltpu.VMEM((hd, rows, dh), BF),
            pltpu.VMEM((2 * hd + own, rows, dh), BF),
            pltpu.VMEM((3, own, dh, fwh), F32),
            pltpu.SMEM((hd,), F32),
            pltpu.SMEM((hd,), F32),
            dma((6,)),
            pltpu.VMEM((hd, rows, dh), BF),
            pltpu.VMEM((hd, rows, rows), F32),
            pltpu.VMEM((hd, rows, rows), BF),
            pltpu.VMEM((hd, rows, dh), F32),
            pltpu.VMEM((hd, rows, 1), F32),
            pltpu.VMEM((hd, rows, 1), F32),
            pltpu.VMEM((hd + own, rows, dh), BF),
            pltpu.VMEM((hd + own, rows, dh), BF),
            pltpu.VMEM((hd, rows, dh), F32),
            pltpu.VMEM((GROUPS, own, 3, dh, 2 * fwh), BF),
            pltpu.VMEM((own, 3, dh, fwh), F32),
            pltpu.VMEM((own, 3, dh, fwh), F32),
            pltpu.VMEM((own, 3, dh, fwh), F32),
            pltpu.VMEM((2, fwh, 2 * rows), F32),
            pltpu.VMEM((fwh, 2 * rows), BF),
            pltpu.VMEM((2 * own, 3, dh, fwh), SENT),
            pltpu.VMEM((max(mates - 1, 1), own, 3, dh, fwh), SENT),
            pltpu.VMEM((own, 3, dh, fwh), F32),
            pltpu.VMEM((own, 3, dh, fwh), SENT),
            pltpu.VMEM((own, 3, dh, fwh), SENT),
            pltpu.VMEM((own, 3, dh, fwh), BF),
            pltpu.VMEM((2, own, rows, dh), BF),
            pltpu.VMEM((own, rows, dh), BF),
            pltpu.VMEM((2, 1, rows), F32),
            pltpu.VMEM((2 * nh, 1, rows), F32),
            pltpu.SemaphoreType.REGULAR((max((mates - 1).bit_length(), 1),)),
            pltpu.SemaphoreType.REGULAR((max(nh.bit_length() - 2, 1),)),
            pltpu.SemaphoreType.REGULAR,
            dma(()), dma(()),
            dma(()), dma((own,)),
            dma(()), dma((2 * hd,)),
            dma((own,)), dma((own,)),
            dma((own,)),
            dma((max(mates - 1, 1),)), dma((max(mates - 1, 1), own * 3)),
            dma((mates,)), dma((own * 3,)),
            dma(()),
            dma(()), dma(()),
        ],
        compiler_params=pltpu.CompilerParams(
            collective_id=0, has_side_effects=True, vmem_limit_bytes=56 * 1024 * 1024
        ),
    )(
        queries, key_rows, values, gate_init, up_init, down_init, step_size, head_scale,
    )
    return (scaled * out_gain[None, :]).astype(BF)


def solution(mesh):
    in_specs = (
        P("frame", "head"),
        P("frame", "head"),
        P("frame", "head"),
        P("head", None, None),
        P("head", None, None),
        P("head", None, None),
        P("head"),
        P("head"),
        P("head"),
    )
    return jax.shard_map(
        shards, mesh=mesh, in_specs=in_specs, out_specs=P("frame", "head"), check_vma=False
    )
```
